256 devices in a mesh: row: 32 (over y, z_lo, core), col: 8 (over z_hi, x).
Axes of the slice: x: 4, y: 4, z: 8 (z_hi: 2, z_lo: 4; z = z_hi * 4 + z_lo), core: 2. Of those that a mesh axis runs over, the one named last changes fastest.
Arguments:
- positions: float32 [3, 32, 8, 128], P(None, 'row', 'col'), may hold values from 0 to 12
- species: int32 [32, 8, 128], P('row', 'col'), may hold values from 0 to 5
- counts: int32 [32, 8, 128], P('row', 'col'), may hold values from 32 to 64
- neighbours: int32 [32, 8, 64, 128], P('row', 'col'), may hold values from 0 to 1151
- ghost_index: int32 [32, 8, 8, 128], P('row', 'col'), may hold values from 0 to 127
- wave_numbers: int32 [3, 1000], replicated, may hold values from -6 to 6, as said below
- embedding: float32 [6, 128], replicated, may hold values from -6 to 6
- w_radial: float32 [16, 128], replicated, may hold values from -1.5 to 1.5
- w_mix: float32 [128, 128], replicated, may hold values from -0.5 to 0.5
- w_read: float32 [128, 128], replicated, may hold values from -0.5 to 0.5
- w_out: float32 [128], replicated, may hold values from -0.5 to 0.5
- amplitude: float32 [128], replicated, may hold values from 10 to 100
- kernel_width: float32 [128], replicated, may hold values from 0.5 to 4
- filter_gain: float32 [1000, 128], replicated, may hold values from 0.1 to 1.9
Outputs:
- forces: float32 [3, 32, 8, 128], P(None, 'row', 'col')
- virial: float32 [3, 3], replicated
The draws below stay inside these ranges and needn't reach their ends.
Inputs may be any that keep to these rules, and one draw needn't show every extreme that they name: `wave_numbers`: the first two rows lie in -6 to 6, the third in 1 to 6. `counts`: slots at or beyond an atom's count are padding. `neighbours`: indices into the extended table of step one. `ghost_index`: local atom indices; repeats are allowed.
All inputs are finite; a program needn't handle non-finite values.
Results may differ from the reference program's by a relative error of at most 0.0003.
Values sent between devices are 32-bit elements; how exact they have to be, the bound alone decides.
A program may use at most 64 MiB of HBM per device.

```python
import math
import jax
import jax.numpy as jnp
from jax import lax

C = 128
K = 1000
NB = 64
NRB = 16
SPEC = 6
KMAX = 6
A_DEV = 128
G_DEV = 128
N_ROW = 32
N_COL = 8


def draw_wave_numbers(key, part):
    plane_numbers = jax.random.randint(jax.random.fold_in(key, 11), (2, K), -KMAX, KMAX + 1)
    height_numbers = jax.random.randint(jax.random.fold_in(key, 12), (1, K), 1, KMAX + 1)
    return jnp.concatenate([plane_numbers, height_numbers], axis=0).astype(jnp.int32)


def touch_ends(values, stream_key, smallest, largest):
    spot = [jax.random.randint(jax.random.fold_in(stream_key, axis), (), 0, length) for axis, length in enumerate(values.shape)]
    longest = values.shape.index(max(values.shape))
    neighbour = spot[:longest] + [(spot[longest] + 1) % values.shape[longest]] + spot[longest + 1:]
    return values.at[tuple(spot)].set(smallest).at[tuple(neighbour)].set(largest)


def shard_levels(key, shape, shards, least, largest):
    def one(dim, parts):
        heights = jax.random.uniform(jax.random.fold_in(jax.random.fold_in(key, 6), dim), (parts,), jnp.float32, least / len(shards), largest / len(shards))
        return jnp.repeat(jnp.exp(heights), shape[dim] // parts).reshape((-1,) + (1,) * (len(shape) - dim - 1))

    factor_of = one(*shards[0])
    for cut in shards[1:]:
        factor_of = factor_of * one(*cut)
    return factor_of


def normal_values(own_key, shape, scale, limit, held_as=jnp.bfloat16):
    values = jax.random.normal(own_key, shape, jnp.float32) * scale
    return jnp.minimum(jnp.maximum(values, -limit), limit).astype(held_as)


def setup_inputs(seed: int = 0) -> dict:
    keys = jax.random.split(jax.random.key(seed), 15)
    return {
        "positions": jnp.clip(12.0 * jax.random.uniform(keys[0], (3, N_ROW, N_COL, A_DEV), jnp.float32) ** shard_levels(keys[0], (3, N_ROW, N_COL, A_DEV), ((1, 32), (2, 8)), -0.2, 0.2), 0.0, 12.0),
        "species": touch_ends(jax.random.randint(keys[1], (N_ROW, N_COL, A_DEV), 0, SPEC), jax.random.fold_in(keys[1], 1), 0, SPEC - 1).astype(jnp.int32),
        "counts": touch_ends(jax.random.randint(keys[2], (N_ROW, N_COL, A_DEV), NB // 2, NB + 1), jax.random.fold_in(keys[2], 1), NB // 2, NB).astype(jnp.int32),
        "neighbours": touch_ends(jax.random.randint(keys[3], (N_ROW, N_COL, NB, A_DEV), 0, A_DEV + 8 * G_DEV), jax.random.fold_in(keys[3], 1), 0, (A_DEV + 8 * G_DEV) - 1).astype(jnp.int32),
        "ghost_index": touch_ends(jax.random.randint(keys[4], (N_ROW, N_COL, 8, G_DEV), 0, A_DEV), jax.random.fold_in(keys[4], 1), 0, A_DEV - 1).astype(jnp.int32),
        "wave_numbers": draw_wave_numbers(jax.random.fold_in(keys[14], 71), 0),
        "embedding": normal_values(keys[6], (SPEC, C), 1.0, 6.0, jnp.float32),
        "w_radial": normal_values(keys[7], (NRB, C), NRB ** -0.5, 1.5, jnp.float32),
        "w_mix": normal_values(keys[8], (C, C), C ** -0.5, 0.5, jnp.float32),
        "w_read": normal_values(keys[9], (C, C), C ** -0.5, 0.5, jnp.float32),
        "w_out": normal_values(keys[10], (C,), C ** -0.5, 0.5, jnp.float32),
        "amplitude": jnp.clip(jnp.exp(jax.random.uniform(keys[11], (C,), jnp.float32, math.log(10.0), math.log(100.0))), 10.0, 100.0),
        "kernel_width": jnp.clip(jnp.exp(jax.random.uniform(keys[12], (C,), jnp.float32, math.log(0.5), math.log(4.0))), 0.5, 4.0),
        "filter_gain": jnp.clip(1.0 + 0.18 * jax.random.normal(keys[13], (K, C), jnp.float32), 0.1, 1.9),
    }


CELL_EDGE = 12.0
HEIGHT = 36.0
EXACT = lax.Precision.HIGHEST
DIRECTIONS = ((-1, -1), (-1, 0), (-1, 1), (0, -1), (0, 1), (1, -1), (1, 0), (1, 1))

def radial_rates(count):
    return 0.003 * jnp.exp(math.log(1.6) * jnp.arange(count, dtype=jnp.int32).astype(jnp.float32))

def block_size(count):
    if count % 125 == 0 and count > 125:
        return 125
    return count

def short_range(edge_vectors, own_kinds, edge_kinds, edge_valid, embedding, w_radial, w_mix, w_read, w_out):
    slot_count, atom_count = edge_valid.shape
    species_count = embedding.shape[0]
    decay_rates = radial_rates(w_radial.shape[0])
    group_size = 4 if slot_count % 4 == 0 else 1
    groups = slot_count // group_size
    vector_groups = jnp.moveaxis(edge_vectors.reshape(3, groups, group_size, atom_count), 1, 0)
    kind_groups = edge_kinds.reshape(groups, group_size, atom_count)
    mask_groups = edge_valid.reshape(groups, group_size, atom_count)
    species_ids = jnp.arange(species_count, dtype=jnp.int32)

    def one_group(running, inputs):
        vectors, neighbour_kinds, edge_mask = inputs
        squared = lax.optimization_barrier(jnp.sum(vectors * vectors, axis=0))
        radial_basis = jnp.exp(-decay_rates[:, None, None] * squared[None])
        filters = jnp.einsum('rsa,rc->sac', radial_basis, w_radial, precision=EXACT)
        onehot = (neighbour_kinds[:, :, None] == species_ids[None, None, :]).astype(jnp.float32)
        features = jnp.einsum('sak,kc->sac', onehot, embedding, precision=EXACT)
        return (running + lax.optimization_barrier(jnp.sum(edge_mask[:, :, None] * filters * features, axis=0)), None)
    initial = jnp.zeros((atom_count, w_radial.shape[1]), jnp.float32)
    summed, _unused = lax.scan(jax.checkpoint(one_group), initial, (vector_groups, kind_groups, mask_groups))
    aggregate = summed / slot_count
    own_onehot = (own_kinds[:, None] == species_ids[None, :]).astype(jnp.float32)
    initial_features = jnp.dot(own_onehot, embedding, precision=EXACT)
    updated = initial_features + jax.nn.silu(jnp.dot(aggregate, w_mix, precision=EXACT))
    readout = jax.nn.silu(jnp.dot(updated, w_read, precision=EXACT))
    energy = jnp.sum(jnp.dot(readout, w_out, precision=EXACT))
    return (energy, updated)

def structure_factors(coords, features, wave_vectors):
    wave_count = wave_vectors.shape[1]
    block_width = block_size(wave_count)
    blocks = jnp.moveaxis(wave_vectors.reshape(3, wave_count // block_width, block_width), 1, 0)

    def one_block(wave_block):
        phases = jnp.einsum('xk,xn->kn', wave_block, coords, precision=EXACT)
        return jnp.stack([jnp.dot(jnp.cos(phases), features, precision=EXACT), jnp.dot(jnp.sin(phases), features, precision=EXACT)])
    pieces = lax.map(jax.checkpoint(one_block), blocks)
    return jnp.moveaxis(pieces, 1, 0).reshape(2, wave_count, features.shape[1])

def wave_vectors_of(wave_numbers, row_count, col_count):
    lengths = jnp.array([CELL_EDGE * row_count, CELL_EDGE * col_count, HEIGHT], jnp.float32)
    return 2.0 * math.pi * wave_numbers.astype(jnp.float32) / lengths[:, None]

def ghost_tables(positions, species, ghost_index):
    coord_list = [positions]
    kind_list = [species]
    for order_id, (row_step, col_step) in enumerate(DIRECTIONS):
        source_id = len(DIRECTIONS) - 1 - order_id
        moved_coords = jnp.roll(positions, (-row_step, -col_step), axis=(1, 2))
        moved_kinds = jnp.roll(species, (-row_step, -col_step), axis=(0, 1))
        moved_index = jnp.roll(ghost_index[:, :, source_id, :], (-row_step, -col_step), axis=(0, 1))
        wide_index = jnp.broadcast_to(moved_index[None], (3,) + moved_index.shape)
        picked = jnp.take_along_axis(moved_coords, wide_index, axis=3)
        offset_vec = jnp.array([row_step * CELL_EDGE, col_step * CELL_EDGE, 0.0], jnp.float32)
        coord_list.append(picked + offset_vec[:, None, None, None])
        kind_list.append(jnp.take_along_axis(moved_kinds, moved_index, axis=2))
    return (jnp.concatenate(coord_list, axis=3), jnp.concatenate(kind_list, axis=2))

def total_energy(positions, strain, species, counts, neighbours, ghost_index, wave_numbers, embedding, w_radial, w_mix, w_read, w_out, amplitude, kernel_width, filter_gain):
    ext_coords, ext_kinds = ghost_tables(positions, species, ghost_index)
    device_count = N_ROW * N_COL
    atom_count = positions.shape[3]
    coord_rows = jnp.moveaxis(ext_coords.reshape(3, device_count, -1), 1, 0)
    kind_rows = ext_kinds.reshape(device_count, -1)
    neighbour_rows = neighbours.reshape(device_count, NB, atom_count)
    count_rows = counts.reshape(device_count, atom_count)
    slot_ids = jnp.arange(NB, dtype=jnp.int32)

    def one_device(inputs):
        coords, kind_table, neighbour_ids, live_counts = inputs
        own_coords = coords[:, :atom_count]
        edge_vectors = coords[:, neighbour_ids] - own_coords[:, None, :]
        edge_vectors = edge_vectors + jnp.einsum('xy,ysa->xsa', strain, edge_vectors, precision=EXACT)
        edge_valid = (slot_ids[:, None] < live_counts[None, :]).astype(jnp.float32)
        return short_range(edge_vectors, kind_table[:atom_count], kind_table[neighbour_ids], edge_valid, embedding, w_radial, w_mix, w_read, w_out)
    energies, updated = lax.map(jax.checkpoint(one_device), (coord_rows, kind_rows, neighbour_rows, count_rows))
    row_shift = jnp.arange(N_ROW, dtype=jnp.int32).astype(jnp.float32) * CELL_EDGE
    col_shift = jnp.arange(N_COL, dtype=jnp.int32).astype(jnp.float32) * CELL_EDGE
    offsets = jnp.stack([jnp.broadcast_to(row_shift[:, None], (N_ROW, N_COL)), jnp.broadcast_to(col_shift[None, :], (N_ROW, N_COL)), jnp.zeros((N_ROW, N_COL), jnp.float32)])
    global_coords = positions + offsets[..., None]
    wave_vectors = wave_vectors_of(wave_numbers, N_ROW, N_COL)
    factors = structure_factors(global_coords.reshape(3, -1), updated.reshape(-1, updated.shape[2]), wave_vectors)
    squared_norm = lax.optimization_barrier(jnp.sum(wave_vectors * wave_vectors, axis=0)) - 2.0 * jnp.einsum('xk,xy,yk->k', wave_vectors, strain, wave_vectors, precision=EXACT)
    volume = CELL_EDGE * N_ROW * CELL_EDGE * N_COL * HEIGHT * (1.0 + jnp.trace(strain))
    weights = amplitude[None, :] * filter_gain * jnp.exp(-kernel_width[None, :] * squared_norm[:, None])
    kspace_energy = 0.5 / volume * jnp.sum(weights * (factors[0] * factors[0] + factors[1] * factors[1]))
    return jnp.sum(energies) + kspace_energy

def reference(positions, species, counts, neighbours, ghost_index, wave_numbers, embedding, w_radial, w_mix, w_read, w_out, amplitude, kernel_width, filter_gain):
    strain = jnp.zeros((3, 3), jnp.float32)
    position_grad, strain_grad = jax.grad(total_energy, argnums=(0, 1))(positions, strain, species, counts, neighbours, ghost_index, wave_numbers, embedding, w_radial, w_mix, w_read, w_out, amplitude, kernel_width, filter_gain)
    volume = CELL_EDGE * N_ROW * CELL_EDGE * N_COL * HEIGHT
    return (-position_grad, -strain_grad / volume)
```

```python
import functools
import math

import jax
import jax.numpy as jnp
from jax import lax
from jax.experimental import pallas as pl
from jax.experimental.pallas import tpu as pltpu
from jax.sharding import PartitionSpec as P

CELL_EDGE = 12.0
HEIGHT = 36.0
ROWS = 32
COLS = 8
VOLUME = CELL_EDGE * ROWS * CELL_EDGE * COLS * HEIGHT
LENGTHS = (CELL_EDGE * ROWS, CELL_EDGE * COLS, HEIGHT)
DIRECTIONS = ((-1, -1), (-1, 0), (-1, 1), (0, -1), (0, 1), (1, -1), (1, 0), (1, 1))
RATE = 0.003
GROWTH = 1.6
BASIS = 16
SPECIES = 6
SLOTS = 64
WAVES = 1000
HIGH = lax.Precision.HIGH
HIGHEST = lax.Precision.HIGHEST
MESH = pl.DeviceIdType.MESH
F32 = jnp.float32
BF16 = jnp.bfloat16
SINE = (
    6.2831854820251465,
    -41.34170150756836,
    81.60513305664062,
    -76.70301818847656,
    42.02592849731445,
    -14.899847030639648,
    3.2381374835968018,
)
COSINE = (
    1.0,
    -19.73920440673828,
    64.93911743164062,
    -85.45014190673828,
    60.16762924194336,
    -25.967599868774414,
    6.528658390045166,
)
N_COPIES = 90


def dot(a, b, ca, cb, precision=None):
    return lax.dot_general(
        a, b, (((ca,), (cb,)), ((), ())), precision=precision, preferred_element_type=F32
    )


def horner(coefs, w):
    value = jnp.full_like(w, coefs[-1])
    for c in coefs[-2::-1]:
        value = value * w + c
    return value


def halves(x):
    hi = x.astype(BF16)
    lo = (x - hi.astype(F32)).astype(BF16)
    return hi, lo


def iota(shape, dim):
    return lax.broadcasted_iota(jnp.int32, shape, dim)


def kernel(
    pos, spec, cnt, nbr, gidx, wn, emb, wrad, wmix, wread, wout, amp, width, gain,
    force, virial,
    own, gsend, pages, gback, gret,
    nmat, umat, tab, emb8, w2,
    vec, kinds, dist, expo, basis, upd, dsilu, gshort,
    fsend, core_in, sums, in_a, in_b, part_a, part_b, in_a2, in_b2, zin, zbuf,
    c3, c2a, c2b, coef, fgrad, cgrad, vgrad, tgrad, vz, vy, vx, vq, vtile,
    ssem, rsem,
):
    row = lax.axis_index("row")
    col = lax.axis_index("col")
    q = lax.rem(row, 2)
    zl = lax.rem(lax.div(row, 2), 4)
    y = lax.div(row, 8)
    x = lax.rem(col, 4)
    zh = lax.div(col, 4)
    z = zh * 4 + zl

    def device(q, x, y, z):
        return (y * 8 + lax.rem(z, 4) * 2 + q, lax.div(z, 4) * 4 + x)

    ghosts = [
        (lax.rem(row + a + ROWS, ROWS), lax.rem(col + b + COLS, COLS)) for a, b in DIRECTIONS
    ]
    partner = device(1 - q, x, y, z)

    def along_x(off):
        return device(q, lax.rem(x + off, 4), y, z)

    def along_y(off):
        return device(q, x, lax.rem(y + off, 4), z)

    def along_z(off):
        return device(q, x, y, lax.rem(z + off, 8))

    def before(i, off, n):
        return lax.rem(i + n - off, n)

    def after(i, off, n):
        return lax.rem(i + off, n)

    barrier = pltpu.get_barrier_semaphore()
    greeted = (
        ghosts
        + [partner]
        + [along_x(off) for off in (1, 2, 3)]
        + [along_y(off) for off in (1, 2, 3)]
        + [along_z(off) for off in range(1, 8)]
    )
    for who in greeted:
        pl.semaphore_signal(barrier, inc=1, device_id=who, device_id_type=MESH)

    started = []

    def send(src, dst, landing, who):
        i = len(started)
        copy = pltpu.make_async_remote_copy(
            src_ref=src,
            dst_ref=dst,
            send_sem=ssem.at[i],
            recv_sem=rsem.at[i],
            device_id=who,
            device_id_type=MESH,
        )
        copy.start()
        started.append(copy)
        return pltpu.make_async_remote_copy(
            src_ref=src,
            dst_ref=landing,
            send_sem=ssem.at[i],
            recv_sem=rsem.at[i],
            device_id=who,
            device_id_type=MESH,
        )

    own[...] = jnp.zeros((8, 128), F32)
    for d in range(3):
        own[d : d + 1, :] = pos[d, 0]
    own[3:4, :] = spec[0].astype(F32)
    table = own[...]
    for d in range(8):
        index = jnp.broadcast_to(gidx[0, 0, d : d + 1, :], (8, 128))
        gsend[d] = jnp.take_along_axis(table, index, axis=1, mode="promise_in_bounds")
    pages[0] = table

    pl.semaphore_wait(barrier, len(greeted))
    waits = [
        send(gsend.at[d], pages.at[8 - d], pages.at[8 - d], ghosts[d]) for d in range(8)
    ]

    gback[...] = jnp.zeros((8, 8, 128), F32)
    nmat[...] = jnp.zeros((16, 1024), F32)
    numbers = wn[...].astype(F32)
    for part in range(3):
        nmat[3 * part : 3 * part + 3, 0:WAVES] = numbers
    umat[...] = jnp.zeros((16, 128), F32)
    offset = (row.astype(F32) * CELL_EDGE, col.astype(F32) * CELL_EDGE, 0.0)
    for d in range(3):
        turn = (pos[d, 0] + offset[d]) * (1.0 / LENGTHS[d])
        for part in range(3):
            piece = turn.astype(BF16).astype(F32)
            umat[3 * part + d : 3 * part + d + 1, :] = piece
            turn = turn - piece
    fractions = umat[...].astype(BF16)

    def trig(i, carry):
        at = pl.multiple_of(i * 128, 128)
        block = nmat[:, pl.ds(at, 128)].astype(BF16)
        turns = dot(block, fractions, 0, 0)
        turns = turns - jnp.floor(turns + 0.5)
        w = turns * turns
        tab[0, pl.ds(at, 128), :] = horner(COSINE, w)
        tab[1, pl.ds(at, 128), :] = horner(SINE, w) * turns
        return carry

    lax.fori_loop(0, 8, trig, 0)
    emb8[...] = jnp.zeros((8, 128), F32)
    emb8[0:SPECIES, :] = emb[...]
    kinds8 = emb8[...]
    for r in range(BASIS):
        w2[8 * r : 8 * r + 8, :] = wrad[r : r + 1, :] * kinds8 * (1.0 / SLOTS)
    onehot = (spec[0] == iota((8, 128), 0)).astype(F32)
    start = dot(onehot, kinds8, 0, 0, HIGHEST)

    for w in waits:
        w.wait_recv()
    live = cnt[0]
    rows8 = iota((8, 128), 0)

    def edge(g, carry):
        at = pl.multiple_of(g * 8, 8)
        index = nbr[0, 0, pl.ds(at, 8), :]
        page = lax.shift_right_logical(index, 7)
        lane = lax.bitwise_and(index, 127)
        picked = [jnp.zeros((8, 128), F32)] * 4
        for p in range(9):
            here = page == p
            for d in range(4):
                line = pages[p, d : d + 1, :]
                if p > 0 and d < 2 and DIRECTIONS[p - 1][d]:
                    line = line + CELL_EDGE * DIRECTIONS[p - 1][d]
                found = jnp.take_along_axis(
                    jnp.broadcast_to(line, (8, 128)), lane, axis=1, mode="promise_in_bounds"
                )
                picked[d] = jnp.where(here, found, picked[d])
        square = jnp.zeros((8, 128), F32)
        for d in range(3):
            v = picked[d] - pos[d, 0]
            vec[d, pl.ds(at, 8), :] = v
            square = square + v * v
        dist[pl.ds(at, 8), :] = square
        kinds[pl.ds(at, 8), :] = jnp.where(rows8 + at < live, picked[3], -1.0)
        return carry

    lax.fori_loop(0, 8, edge, 0)

    def radial(r, rate):
        e = jnp.exp(dist[...] * (-rate))
        expo[r] = e
        k = kinds[...]
        tile = jnp.zeros((8, 128), F32)
        for s in range(SPECIES):
            total = jnp.sum(jnp.where(k == s, e, 0.0), axis=0, keepdims=True)
            tile = jnp.where(rows8 == s, total, tile)
        basis[pl.ds(pl.multiple_of(r * 8, 8), 8), :] = tile
        return rate * GROWTH

    lax.fori_loop(0, BASIS, radial, jnp.float32(RATE))

    aggregate = dot(basis[...], w2[...], 0, 0, HIGH)
    u = dot(aggregate, wmix[...], 1, 0, HIGH)
    gate = 1.0 / (1.0 + jnp.exp(-u))
    upd[...] = start + u * gate
    dsilu[...] = gate * (1.0 + u * (1.0 - gate))

    def factor(half, i):
        return dot(tab[half, 128 * i : 128 * i + 128, :], upd[...], 1, 0, HIGH)

    waits = []
    for i in range(8):
        at = slice(128 * i, 128 * i + 128)
        fsend[at, :] = factor(1 - q, i)
        waits.append(send(fsend.at[at], core_in.at[at], core_in.at[at], partner))
    for i in range(8):
        at = slice(128 * i, 128 * i + 128)
        mine = factor(q, i)
        waits[i].wait_recv()
        sums[at, :] = mine + core_in[at, :]

    waits_a, waits_b = [], []
    for off in (2, 1, 3):
        at = pl.ds(pl.multiple_of(after(x, off, 4) * 128, 128), 128)
        waits_a.append(send(sums.at[at], in_a.at[off - 1], in_a.at[off - 1], along_x(off)))
        at = pl.ds(pl.multiple_of(512 + after(y, off, 4) * 128, 128), 128)
        waits_b.append(send(sums.at[at], in_b.at[off - 1], in_b.at[off - 1], along_y(off)))
    p = dot(upd[...], wread[...], 1, 0, HIGH)
    gate = 1.0 / (1.0 + jnp.exp(-p))
    gshort[...] = dot(wout[...] * (gate * (1.0 + p * (1.0 - gate))), wread[...], 1, 1, HIGH)

    for w in waits_a:
        w.wait_recv()
    part_a[...] = sums[pl.ds(pl.multiple_of(x * 128, 128), 128), :] + in_a[0] + in_a[1] + in_a[2]
    waits_a2, waits_b2 = [], []
    for off in (2, 1, 3):
        at = pl.ds(pl.multiple_of(after(y, off, 4) * 32, 32), 32)
        waits_a2.append(send(part_a.at[at], in_a2.at[off - 1], in_a2.at[off - 1], along_y(off)))
    for w in waits_b:
        w.wait_recv()
    part_b[...] = (
        sums[pl.ds(pl.multiple_of(512 + y * 128, 128), 128), :] + in_b[0] + in_b[1] + in_b[2]
    )
    for off in (2, 1, 3):
        at = pl.ds(pl.multiple_of(after(x, off, 4) * 32, 32), 32)
        waits_b2.append(send(part_b.at[at], in_b2.at[off - 1], in_b2.at[off - 1], along_x(off)))
    for w in waits_a2:
        w.wait_recv()
    zbuf[0:32, :] = (
        part_a[pl.ds(pl.multiple_of(y * 32, 32), 32), :] + in_a2[0] + in_a2[1] + in_a2[2]
    )
    for w in waits_b2:
        w.wait_recv()
    zbuf[32:64, :] = (
        part_b[pl.ds(pl.multiple_of(x * 32, 32), 32), :] + in_b2[0] + in_b2[1] + in_b2[2]
    )
    waits = []
    for off in (4, 3, 5, 2, 6, 1, 7):
        at = pl.ds(pl.multiple_of(after(z, off, 8) * 8, 8), 8)
        waits.append(send(zbuf.at[at], zin.at[off - 1], zin.at[off - 1], along_z(off)))

    first = (1 - zh) * (128 * x + 32 * y) + zh * (512 + 128 * y + 32 * x) + 8 * zl
    chosen = (iota((8, 1024), 1) == iota((8, 1024), 0) + first).astype(BF16)
    mine = dot(chosen, nmat[...].astype(BF16), 1, 1)
    k_of = [mine[:, d : d + 1] * (2.0 * math.pi / LENGTHS[d]) for d in range(3)]
    norm = k_of[0] * k_of[0] + k_of[1] * k_of[1] + k_of[2] * k_of[2]
    inside = lax.div(first, WAVES)
    source = pl.multiple_of(first - inside * WAVES, 8)
    weight = amp[...] * gain[pl.ds(source, 8), :] * jnp.exp(-width[...] * norm)
    weight = jnp.where(rows8 + first < WAVES, weight * (1.0 / VOLUME), 0.0)

    for w in waits:
        w.wait_recv()
    total = zbuf[pl.ds(pl.multiple_of(z * 8, 8), 8), :]
    for i in range(7):
        total = total + zin[i]
    result = weight * total
    mine_z = pl.ds(pl.multiple_of(z * 8, 8), 8)
    c3[mine_z, :] = result
    waits = []
    for off in (4, 3, 5, 2, 6, 1, 7):
        at = pl.ds(pl.multiple_of(before(z, off, 8) * 8, 8), 8)
        waits.append(send(c3.at[mine_z], c3.at[mine_z], c3.at[at], along_z(off)))

    power = result * total
    strain = jnp.sum(width[...] * power, axis=1, keepdims=True)
    energy = 0.5 * jnp.sum(jnp.sum(power, axis=1, keepdims=True), axis=0, keepdims=True)
    rows_v = iota((8, 128), 0)
    lanes_v = iota((8, 128), 1)
    tile = jnp.where((rows_v == lanes_v) & (rows_v < 3), energy, 0.0)
    for a in range(3):
        for b in range(a, 3):
            s = jnp.sum(k_of[a] * k_of[b] * strain, axis=0, keepdims=True)
            there = (rows_v == a) & (lanes_v == b)
            if a != b:
                there = there | ((rows_v == b) & (lanes_v == a))
            tile = tile - jnp.where(there, s, 0.0)
    vtile[...] = tile

    fgrad[...] = gshort[...]
    cgrad[...] = jnp.zeros((16, 128), F32)

    for w in waits:
        w.wait_recv()
    waits_a, waits_b = [], []
    mine_a = pl.ds(pl.multiple_of(y * 32, 32), 32)
    mine_b = pl.ds(pl.multiple_of(x * 32, 32), 32)
    for off in (2, 1, 3):
        at = pl.ds(pl.multiple_of(before(y, off, 4) * 32, 32), 32)
        waits_a.append(send(c3.at[0:32], c2a.at[mine_a], c2a.at[at], along_y(off)))
        at = pl.ds(pl.multiple_of(before(x, off, 4) * 32, 32), 32)
        waits_b.append(send(c3.at[32:64], c2b.at[mine_b], c2b.at[at], along_x(off)))
    c2a[mine_a, :] = c3[0:32, :]
    c2b[mine_b, :] = c3[32:64, :]

    chunk_a = pl.ds(pl.multiple_of(x * 128, 128), 128)
    chunk_b = pl.ds(pl.multiple_of(512 + y * 128, 128), 128)
    arrivals = []
    for w in waits_a:
        w.wait_recv()
    for off in (2, 1, 3):
        at = pl.ds(pl.multiple_of(before(x, off, 4) * 128, 128), 128)
        arrivals.append((send(c2a, coef.at[q, chunk_a], coef.at[q, at], along_x(off)), at))
    shared = [(send(c2a, coef.at[q, chunk_a], coef.at[1 - q, chunk_a], partner), chunk_a)]
    coef[q, chunk_a, :] = c2a[...]
    for w in waits_b:
        w.wait_recv()
    for off in (2, 1, 3):
        at = pl.ds(pl.multiple_of(512 + before(y, off, 4) * 128, 128), 128)
        arrivals.append((send(c2b, coef.at[q, chunk_b], coef.at[q, at], along_y(off)), at))
    shared.append((send(c2b, coef.at[q, chunk_b], coef.at[1 - q, chunk_b], partner), chunk_b))
    coef[q, chunk_b, :] = c2b[...]

    def back(half, sign, at):
        c = coef[half, at, :]
        fgrad[...] += dot(tab[half, at, :], c, 0, 0, HIGH)
        turned = dot(c, upd[...], 1, 1, HIGH) * tab[1 - half, at, :] * sign
        cgrad[...] += dot(nmat[:, at], turned, 1, 0, HIGH)

    sign_q = (2 * q - 1).astype(F32)
    back(q, sign_q, chunk_a)
    back(q, sign_q, chunk_b)
    for i in (1, 4, 2, 5, 0, 3):
        w, at = arrivals[i]
        w.wait_recv()
        shared.append((send(coef.at[q, at], coef.at[q, at], coef.at[1 - q, at], partner), at))
        back(q, sign_q, at)
    for w, at in shared:
        w.wait_recv()
        back(1 - q, -sign_q, at)

    du = fgrad[...] * dsilu[...]
    daggregate = dot(du, wmix[...], 1, 1, HIGH)
    basis[...] = dot(w2[...], daggregate, 1, 1, HIGH)

    def radial_back(r, carry):
        rate, grad = carry
        d = basis[pl.ds(pl.multiple_of(r * 8, 8), 8), :] * (-2.0 * rate)
        k = kinds[...]
        chosen = jnp.zeros((SLOTS, 128), F32)
        for s in range(SPECIES):
            chosen = jnp.where(k == s, d[s : s + 1, :], chosen)
        return rate * GROWTH, grad + chosen * expo[r]

    _, slope = lax.fori_loop(
        0, BASIS, radial_back, (jnp.float32(RATE), jnp.zeros((SLOTS, 128), F32))
    )
    spent = []
    for d in range(3):
        g = slope * vec[d]
        vgrad[d] = g
        spent.append(jnp.sum(g, axis=0, keepdims=True))
    tile = vtile[...]
    for a in range(3):
        for b in range(a, 3):
            s = jnp.sum(vgrad[a] * vec[b], axis=0, keepdims=True)
            s = jnp.sum(s, axis=1, keepdims=True)
            there = (rows_v == a) & (lanes_v == b)
            if a != b:
                there = there | ((rows_v == b) & (lanes_v == a))
            tile = tile - jnp.where(there, s, 0.0)

    def gather(buffer, value, me, n, to):
        buffer[me] = value
        return [
            send(buffer.at[me], buffer.at[me], buffer.at[before(me, off, n)], to(off))
            for off in range(1, n)
        ]

    def add_up(buffer, n):
        value = buffer[0]
        for i in range(1, n):
            value = value + buffer[i]
        return value

    waits_v = gather(vz, tile, z, 8, along_z)

    rows16 = iota((16, 128), 0)
    rows128 = iota((128, 128), 0)

    def scatter(g, total):
        left, right = [], []
        for s in range(4):
            at = pl.ds(g * 4 + s, 1)
            index = nbr[0, 0, at, :]
            page = lax.shift_right_logical(index, 7)
            lane = lax.bitwise_and(index, 127)
            right.append((rows128 == lane).astype(F32).astype(BF16))
            lines = jnp.concatenate(
                [jnp.where(rows16 == page, vgrad[d, at, :], 0.0) for d in range(3)], axis=0
            )
            left.append(jnp.concatenate(halves(lines), axis=0))
        return total + dot(
            jnp.concatenate(left, axis=1), jnp.concatenate(right, axis=1), 1, 1
        )

    total = lax.fori_loop(0, SLOTS // 4, scatter, jnp.zeros((96, 128), F32))
    tgrad[...] = total[0:48, :] + total[48:96, :]
    for p in range(8):
        for d in range(3):
            gback[p, d : d + 1, :] = tgrad[16 * d + p + 1 : 16 * d + p + 2, :]
    waits_g = [send(gback.at[p], gret.at[7 - p], gret.at[7 - p], ghosts[p]) for p in range(8)]

    for w in waits_v:
        w.wait_recv()
    waits_v = gather(vy, add_up(vz, 8), y, 4, along_y)
    left, right = [], []
    for d in range(8):
        right.append((rows128 == gidx[0, 0, d : d + 1, :]).astype(F32).astype(BF16))
    for w in waits_v:
        w.wait_recv()
    waits_v = gather(vx, add_up(vy, 4), x, 4, along_x)
    for w in waits_g:
        w.wait_recv()
    for d in range(8):
        hi, lo = halves(jnp.concatenate([gret[d], jnp.zeros((8, 128), F32)], axis=0))
        left.append(jnp.concatenate([hi, lo], axis=0))
    back_home = dot(jnp.concatenate(left, axis=1), jnp.concatenate(right, axis=1), 1, 1)
    back_home = back_home[0:16, :] + back_home[16:32, :]
    moved = cgrad[...]
    for d in range(3):
        grad = (
            tgrad[16 * d : 16 * d + 1, :]
            - spent[d]
            + moved[d : d + 1, :] * (2.0 * math.pi / LENGTHS[d])
            + back_home[d : d + 1, :]
        )
        force[d, 0] = -grad
    for w in waits_v:
        w.wait_recv()
    waits_v = gather(vq, add_up(vx, 4), q, 2, lambda off: partner)
    for w in waits_v:
        w.wait_recv()
    virial[...] = (add_up(vq, 2) * (1.0 / VOLUME))[0:3, 0:3]
    for copy in started:
        copy.wait_send()


def scratch():
    shapes = [
        (8, 128), (8, 8, 128), (9, 8, 128), (8, 8, 128), (8, 8, 128),
        (16, 1024), (16, 128), (2, 1024, 128), (8, 128), (128, 128),
        (3, 64, 128), (64, 128), (64, 128), (16, 64, 128), (128, 128),
        (128, 128), (128, 128), (128, 128),
        (1024, 128), (1024, 128), (1024, 128), (3, 128, 128), (3, 128, 128),
        (128, 128), (128, 128), (3, 32, 128), (3, 32, 128), (7, 8, 128), (64, 128),
        (64, 128), (128, 128), (128, 128), (2, 1024, 128), (128, 128), (16, 128),
        (3, 64, 128), (48, 128), (8, 8, 128), (4, 8, 128), (4, 8, 128), (2, 8, 128),
        (8, 128),
    ]
    return [pltpu.VMEM(s, F32) for s in shapes] + [
        pltpu.SemaphoreType.DMA((N_COPIES,)),
        pltpu.SemaphoreType.DMA((N_COPIES,)),
    ]


def per_device(
    positions, species, counts, neighbours, ghost_index, wave_numbers, embedding,
    w_radial, w_mix, w_read, w_out, amplitude, kernel_width, filter_gain,
):
    whole = pl.BlockSpec(memory_space=pltpu.VMEM)
    return pl.pallas_call(
        kernel,
        out_shape=(
            jax.ShapeDtypeStruct(positions.shape, F32),
            jax.ShapeDtypeStruct((3, 3), F32),
        ),
        in_specs=[whole] * 14,
        out_specs=(whole, whole),
        scratch_shapes=scratch(),
        compiler_params=pltpu.CompilerParams(collective_id=0, has_side_effects=True),
        name="ewald",
    )(
        positions, species, counts, neighbours, ghost_index, wave_numbers, embedding,
        w_radial, w_mix, w_read, w_out.reshape(1, 128), amplitude.reshape(1, 128),
        kernel_width.reshape(1, 128), filter_gain,
    )


def solution(mesh):
    return jax.shard_map(
        per_device,
        mesh=mesh,
        in_specs=(
            P(None, "row", "col", None),
            P("row", "col", None),
            P("row", "col", None),
            P("row", "col", None, None),
            P("row", "col", None, None),
            P(), P(), P(), P(), P(), P(), P(), P(), P(),
        ),
        out_specs=(P(None, "row", "col", None), P()),
        check_vma=False,
    )
```

```python
import functools
import math

import jax
import jax.numpy as jnp
from jax import lax
from jax.experimental import pallas as pl
from jax.experimental.pallas import tpu as pltpu
from jax.sharding import PartitionSpec as P

CELL_EDGE = 12.0
HEIGHT = 36.0
ROWS = 32
COLS = 8
VOLUME = CELL_EDGE * ROWS * CELL_EDGE * COLS * HEIGHT
LENGTHS = (CELL_EDGE * ROWS, CELL_EDGE * COLS, HEIGHT)
DIRECTIONS = ((-1, -1), (-1, 0), (-1, 1), (0, -1), (0, 1), (1, -1), (1, 0), (1, 1))
RATE = 0.003
GROWTH = 1.6
BASIS = 16
SPECIES = 6
SLOTS = 64
WAVES = 1000
HIGH = lax.Precision.HIGH
HIGHEST = lax.Precision.HIGHEST
MESH = pl.DeviceIdType.MESH
F32 = jnp.float32
BF16 = jnp.bfloat16
SINE = (
    6.2831854820251465,
    -41.34170150756836,
    81.60513305664062,
    -76.70301818847656,
    42.02592849731445,
    -14.899847030639648,
    3.2381374835968018,
)
COSINE = (
    1.0,
    -19.73920440673828,
    64.93911743164062,
    -85.45014190673828,
    60.16762924194336,
    -25.967599868774414,
    6.528658390045166,
)
def dot(a, b, ca, cb, precision=None):
    return lax.dot_general(
        a, b, (((ca,), (cb,)), ((), ())), precision=precision, preferred_element_type=F32
    )


def horner(coefs, w):
    value = jnp.full_like(w, coefs[-1])
    for c in coefs[-2::-1]:
        value = value * w + c
    return value


def halves(x):
    hi = x.astype(BF16)
    lo = (x - hi.astype(F32)).astype(BF16)
    return hi, lo


def iota(shape, dim):
    return lax.broadcasted_iota(jnp.int32, shape, dim)


N_COPIES = 130
INPUTS = (
    ((3, 1, 1, 128), F32), ((1, 1, 128), jnp.int32), ((1, 1, 128), jnp.int32),
    ((1, 1, 64, 128), jnp.int32), ((1, 1, 8, 128), jnp.int32), ((3, 1000), jnp.int32),
    ((6, 128), F32), ((16, 128), F32), ((128, 128), F32), ((128, 128), F32), ((1, 128), F32),
    ((1, 128), F32), ((1, 128), F32), ((1000, 128), F32),
)
SCRATCH = (
    ("own", (8, 128), F32), ("mate", (8, 128), F32), ("gsend", (8, 8, 128), F32),
    ("pages", (9, 8, 128), F32), ("gback", (8, 8, 128), F32), ("gret", (8, 8, 128), F32),
    ("nmat", (16, 1024), F32), ("umat", (16, 256), F32), ("tab", (2, 4, 128, 256), F32),
    ("tsplit", (2, 4, 128, 768), BF16), ("tturn", (2, 4, 256, 384), BF16),
    ("emb8", (8, 128), F32), ("w2", (128, 128), F32),
    ("vec", (3, 64, 128), F32), ("kinds", (64, 128), F32), ("dist", (64, 128), F32),
    ("expo", (16, 64, 128), F32), ("basis", (128, 128), F32), ("upd", (256, 128), F32),
    ("usplit", (768, 128), BF16), ("uturn", (384, 256), BF16),
    ("dsilu", (128, 128), F32), ("gshort", (128, 128), F32),
    ("sums", (2, 4, 4, 32, 128), F32), ("in1", (2, 3, 4, 32, 128), F32),
    ("part", (2, 4, 32, 128), F32), ("in2", (2, 3, 32, 128), F32),
    ("zin", (7, 8, 128), F32), ("zbuf", (64, 128), F32), ("c3", (64, 128), F32),
    ("coef", (2, 4, 4, 32, 128), F32), ("fgrad", (256, 128), F32), ("cgrad", (16, 256), F32),
    ("xout", (144, 128), F32), ("xin", (144, 128), F32),
    ("marks", (16, 128, 512), BF16), ("gmarks", (128, 1024), BF16),
    ("vgrad", (3, 64, 128), F32), ("tgrad", (48, 128), F32),
    ("va", (16, 8, 128), F32), ("vb", (16, 8, 128), F32),
)


def kernel(*refs):
    ins, out = refs[:14], refs[14]
    here = refs[15:29]
    named = refs[29 : 29 + len(SCRATCH)]
    ssem, rsem, lsem = refs[29 + len(SCRATCH) :]
    (pos, spec, cnt, nbr, gidx, wn, emb, wrad, wmix, wread, wout, amp, width, gain) = here
    (
        own, mate, gsend, pages, gback, gret, nmat, umat, tab, tsplit, tturn, emb8, w2,
        vec, kinds, dist, expo, basis, upd, usplit, uturn, dsilu, gshort,
        sums, in1, part, in2, zin, zbuf, c3, coef, fgrad, cgrad, xout, xin,
        marks, gmarks, vgrad, tgrad, va, vb,
    ) = named
    row = lax.axis_index("row")
    col = lax.axis_index("col")
    q = lax.rem(row, 2)
    zl = lax.rem(lax.div(row, 2), 4)
    y = lax.div(row, 8)
    x = lax.rem(col, 4)
    zh = lax.div(col, 4)
    z = zh * 4 + zl

    def device(q, x, y, z):
        return (y * 8 + lax.rem(z, 4) * 2 + q, lax.div(z, 4) * 4 + x)

    ghosts = [
        (lax.rem(row + a + ROWS, ROWS), lax.rem(col + b + COLS, COLS)) for a, b in DIRECTIONS
    ]
    partner = device(1 - q, x, y, z)

    def along_x(off):
        return device(q, lax.rem(x + off, 4), y, z)

    def along_y(off):
        return device(q, x, lax.rem(y + off, 4), z)

    def along_z(off):
        return device(q, x, y, lax.rem(z + off, 8))

    m_zq = z * 2 + q
    m_xy = x * 4 + y

    def among_zq(off):
        m = lax.rem(m_zq + off, 16)
        return device(lax.rem(m, 2), x, y, lax.div(m, 2))

    def among_xy(off):
        m = lax.rem(m_xy + off, 16)
        return device(q, lax.div(m, 4), lax.rem(m, 4), z)

    def before(i, off, n):
        return lax.rem(i + n - off, n)

    def after(i, off, n):
        return lax.rem(i + off, n)

    barrier = pltpu.get_barrier_semaphore()
    greeted = (
        ghosts
        + [among_zq(off) for off in range(1, 16)]
        + [among_xy(off) for off in range(1, 16)]
    )
    for who in greeted:
        pl.semaphore_signal(barrier, inc=1, device_id=who, device_id_type=MESH)
    loads = [pltpu.make_async_copy(ins[i], here[i], lsem.at[i]) for i in range(14)]
    for copy in loads:
        copy.start()

    started = []

    def send(src, dst, landing, who):
        i = len(started)
        copy = pltpu.make_async_remote_copy(
            src_ref=src,
            dst_ref=dst,
            send_sem=ssem.at[i],
            recv_sem=rsem.at[i],
            device_id=who,
            device_id_type=MESH,
        )
        copy.start()
        started.append(copy)
        return pltpu.make_async_remote_copy(
            src_ref=src,
            dst_ref=landing,
            send_sem=ssem.at[i],
            recv_sem=rsem.at[i],
            device_id=who,
            device_id_type=MESH,
        )

    gback[...] = jnp.zeros((8, 8, 128), F32)
    nmat[...] = jnp.zeros((16, 1024), F32)
    umat[...] = jnp.zeros((16, 256), F32)
    emb8[...] = jnp.zeros((8, 128), F32)
    own[...] = jnp.zeros((8, 128), F32)
    for copy in loads:
        copy.wait()

    for d in range(3):
        own[d : d + 1, :] = pos[d, 0]
    own[3:4, :] = spec[0].astype(F32)
    table = own[...]
    for d in range(8):
        index = jnp.broadcast_to(gidx[0, 0, d : d + 1, :], (8, 128))
        gsend[d] = jnp.take_along_axis(table, index, axis=1, mode="promise_in_bounds")
    pages[0] = table
    numbers = wn[...].astype(F32)
    for p in range(3):
        nmat[3 * p : 3 * p + 3, 0:WAVES] = numbers

    pl.semaphore_wait(barrier, len(greeted))
    wait_mate = send(own, mate, mate, partner)
    waits = [
        send(gsend.at[d], pages.at[8 - d], pages.at[8 - d], ghosts[d]) for d in range(8)
    ]

    emb8[0:SPECIES, :] = emb[...]
    kinds8 = emb8[...]
    for r in range(BASIS):
        w2[8 * r : 8 * r + 8, :] = wrad[r : r + 1, :] * kinds8 * (1.0 / SLOTS)
    onehot = (spec[0] == iota((8, 128), 0)).astype(F32)
    start = dot(onehot, kinds8, 0, 0, HIGHEST)

    wait_mate.wait_recv()
    column = col.astype(F32) * CELL_EDGE
    offsets = (
        (row.astype(F32) * CELL_EDGE, column, 0.0),
        ((row + 1 - 2 * q).astype(F32) * CELL_EDGE, column, 0.0),
    )
    for side, ref in enumerate((own, mate)):
        for d in range(3):
            turn = (ref[d : d + 1, :] + offsets[side][d]) * (1.0 / LENGTHS[d])
            for p in range(3):
                piece = turn.astype(BF16).astype(F32)
                umat[3 * p + d : 3 * p + d + 1, 128 * side : 128 * side + 128] = piece
                turn = turn - piece
    fractions = umat[...].astype(BF16)

    def trig(i, carry):
        block = nmat[:, pl.ds(pl.multiple_of(q * 512 + i * 128, 128), 128)].astype(BF16)
        turns = dot(block, fractions, 0, 0)
        turns = turns - jnp.floor(turns + 0.5)
        w = turns * turns
        for f, value in enumerate((horner(COSINE, w), horner(SINE, w) * turns)):
            tab[f, i] = value
            hi, lo = halves(value)
            for side in range(2):
                mine = slice(128 * side, 128 * side + 128)
                for p, half in enumerate((hi, lo, hi)):
                    at = 384 * side + 128 * p
                    tsplit[f, i, :, at : at + 128] = half[:, mine]
        turns = dot(fractions, block, 0, 0)
        turns = turns - jnp.floor(turns + 0.5)
        w = turns * turns
        for f, value in enumerate((horner(COSINE, w), horner(SINE, w) * turns)):
            hi, lo = halves(value)
            for p, half in enumerate((hi, lo, hi)):
                tturn[f, i, :, 128 * p : 128 * p + 128] = half
        return carry

    lax.fori_loop(0, 4, trig, 0)

    for w in waits:
        w.wait_recv()
    live = cnt[0]
    rows8 = iota((8, 128), 0)

    def edge(g, carry):
        at = pl.multiple_of(g * 8, 8)
        index = nbr[0, 0, pl.ds(at, 8), :]
        page = lax.shift_right_logical(index, 7)
        lane = lax.bitwise_and(index, 127)
        picked = [jnp.zeros((8, 128), F32)] * 4
        for p in range(9):
            here = page == p
            for d in range(4):
                line = pages[p, d : d + 1, :]
                if p > 0 and d < 2 and DIRECTIONS[p - 1][d]:
                    line = line + CELL_EDGE * DIRECTIONS[p - 1][d]
                found = jnp.take_along_axis(
                    jnp.broadcast_to(line, (8, 128)), lane, axis=1, mode="promise_in_bounds"
                )
                picked[d] = jnp.where(here, found, picked[d])
        square = jnp.zeros((8, 128), F32)
        for d in range(3):
            v = picked[d] - pos[d, 0]
            vec[d, pl.ds(at, 8), :] = v
            square = square + v * v
        dist[pl.ds(at, 8), :] = square
        kinds[pl.ds(at, 8), :] = jnp.where(rows8 + at < live, picked[3], -1.0)
        return carry

    lax.fori_loop(0, 8, edge, 0)

    def radial(r, rate):
        e = jnp.exp(dist[...] * (-rate))
        expo[r] = e
        k = kinds[...]
        tile = jnp.zeros((8, 128), F32)
        for s in range(SPECIES):
            total = jnp.sum(jnp.where(k == s, e, 0.0), axis=0, keepdims=True)
            tile = jnp.where(rows8 == s, total, tile)
        basis[pl.ds(pl.multiple_of(r * 8, 8), 8), :] = tile
        return rate * GROWTH

    lax.fori_loop(0, BASIS, radial, jnp.float32(RATE))

    aggregate = dot(basis[...], w2[...], 0, 0, HIGH)
    u = dot(aggregate, wmix[...], 1, 0, HIGH)
    gate = 1.0 / (1.0 + jnp.exp(-u))
    mine = start + u * gate
    upd[0:128, :] = mine
    wait_mate = send(upd.at[0:128], upd.at[128:256], upd.at[128:256], partner)
    dsilu[...] = gate * (1.0 + u * (1.0 - gate))
    p = dot(mine, wread[...], 1, 0, HIGH)
    gate = 1.0 / (1.0 + jnp.exp(-p))
    gshort[...] = dot(wout[...] * (gate * (1.0 + p * (1.0 - gate))), wread[...], 1, 1, HIGH)

    def split(side):
        value = upd[128 * side : 128 * side + 128, :]
        hi, lo = halves(value)
        for p, half in enumerate((hi, hi, lo)):
            usplit[384 * side + 128 * p : 384 * side + 128 * p + 128, :] = half
        hi, lo = halves(value.T)
        for p, half in enumerate((hi, hi, lo)):
            uturn[128 * p : 128 * p + 128, 128 * side : 128 * side + 128] = half

    split(0)
    wait_mate.wait_recv()
    split(1)

    place = (x, y)
    second = (y, x)
    along = (along_x, along_y)
    order = (2, 1, 3, 0)
    waits1 = {}
    for off in order:
        for f in range(2):
            chunk = after(place[f], off, 4)
            value = dot(tsplit[f, chunk], usplit[...], 1, 0)
            sums[f, chunk] = value.reshape(4, 32, 128)
            if off == 0:
                continue
            for off2 in order:
                waits1[f, off, off2] = send(
                    sums.at[f, chunk, after(second[f], off2, 4)],
                    in1.at[f, off - 1, off2],
                    in1.at[f, off - 1, off2],
                    along[f](off),
                )
    waits2 = {}
    for off2 in order:
        for f in range(2):
            for off in (1, 3, 2):
                waits1[f, off, off2].wait_recv()
            total = (
                sums[f, place[f], after(second[f], off2, 4)]
                + in1[f, 0, off2]
                + in1[f, 1, off2]
                + in1[f, 2, off2]
            )
            if off2 == 0:
                zbuf[32 * f : 32 * f + 32, :] = total
                continue
            part[f, off2] = total
            waits2[f, off2] = send(
                part.at[f, off2], in2.at[f, off2 - 1], in2.at[f, off2 - 1], along[1 - f](off2)
            )
    for f in range(2):
        for off2 in (1, 3, 2):
            waits2[f, off2].wait_recv()
        zbuf[32 * f : 32 * f + 32, :] += in2[f, 0] + in2[f, 1] + in2[f, 2]
    waits = []
    for off in (4, 3, 5, 2, 6, 1, 7):
        at = pl.ds(pl.multiple_of(after(z, off, 8) * 8, 8), 8)
        waits.append(send(zbuf.at[at], zin.at[off - 1], zin.at[off - 1], along_z(off)))

    first = 512 * q + (1 - zh) * (128 * x + 32 * y) + zh * (128 * y + 32 * x) + 8 * zl
    chosen = (iota((8, 1024), 1) == iota((8, 1024), 0) + first).astype(BF16)
    mine = dot(chosen, nmat[...].astype(BF16), 1, 1)
    k_of = [mine[:, d : d + 1] * (2.0 * math.pi / LENGTHS[d]) for d in range(3)]
    norm = k_of[0] * k_of[0] + k_of[1] * k_of[1] + k_of[2] * k_of[2]
    inside = lax.div(first, WAVES)
    source = pl.multiple_of(first - inside * WAVES, 8)
    weight = amp[...] * gain[pl.ds(source, 8), :] * jnp.exp(-width[...] * norm)
    weight = jnp.where(rows8 + first < WAVES, weight * (1.0 / VOLUME), 0.0)

    rows128 = iota((128, 128), 0)

    def mark(g, carry):
        for s in range(4):
            lane = lax.bitwise_and(nbr[0, 0, pl.ds(g * 4 + s, 1), :], 127)
            marks[g, :, 128 * s : 128 * s + 128] = (rows128 == lane).astype(F32).astype(BF16)
        return carry

    lax.fori_loop(0, 16, mark, 0)
    for d in range(8):
        gmarks[:, 128 * d : 128 * d + 128] = (
            (rows128 == gidx[0, 0, d : d + 1, :]).astype(F32).astype(BF16)
        )

    for w in waits:
        w.wait_recv()
    total = zbuf[pl.ds(pl.multiple_of(z * 8, 8), 8), :]
    for i in range(7):
        total = total + zin[i]
    result = weight * total
    mine_z = pl.ds(pl.multiple_of(z * 8, 8), 8)
    c3[mine_z, :] = result
    waits = []
    for off in (4, 3, 5, 2, 6, 1, 7):
        at = pl.ds(pl.multiple_of(before(z, off, 8) * 8, 8), 8)
        waits.append(send(c3.at[mine_z], c3.at[mine_z], c3.at[at], along_z(off)))

    power = result * total
    strain = jnp.sum(width[...] * power, axis=1, keepdims=True)
    energy = 0.5 * jnp.sum(jnp.sum(power, axis=1, keepdims=True), axis=0, keepdims=True)
    lanes8 = iota((8, 128), 1)
    tile = jnp.where((rows8 == lanes8) & (rows8 < 3), energy, 0.0)
    for a in range(3):
        for b in range(a, 3):
            s = jnp.sum(k_of[a] * k_of[b] * strain, axis=0, keepdims=True)
            there = (rows8 == a) & (lanes8 == b)
            if a != b:
                there = there | ((rows8 == b) & (lanes8 == a))
            tile = tile - jnp.where(there, s, 0.0)

    fgrad[...] = jnp.zeros((256, 128), F32)
    cgrad[...] = jnp.zeros((16, 256), F32)

    for w in waits:
        w.wait_recv()

    rounds = (1, 3, 2)
    waits2, waits1 = {}, {}

    def spread(f, off2, piece, src):
        for off in (2, 1, 3):
            waits1[f, off, off2] = send(
                src,
                coef.at[f, place[f], piece],
                coef.at[f, before(place[f], off, 4), piece],
                along[f](off),
            )

    for off2 in (2, 1, 3):
        for f in range(2):
            waits2[f, off2] = send(
                c3.at[32 * f : 32 * f + 32],
                coef.at[f, place[f], second[f]],
                coef.at[f, place[f], before(second[f], off2, 4)],
                along[1 - f](off2),
            )
    for f in range(2):
        spread(f, 0, second[f], c3.at[32 * f : 32 * f + 32])
        coef[f, place[f], second[f]] = c3[32 * f : 32 * f + 32, :]
    for off2 in rounds:
        for f in range(2):
            waits2[f, off2].wait_recv()
            piece = before(second[f], off2, 4)
            spread(f, off2, piece, coef.at[f, place[f], piece])

    def back(f, chunk, low, high):
        c = coef[f, chunk].reshape(128, 128)
        hi, lo = halves(c)
        fgrad[low:high, :] += dot(
            tturn[f, chunk, low:high, :], jnp.concatenate([hi, hi, lo], axis=0), 1, 0
        )
        a = dot(jnp.concatenate([hi, lo, hi], axis=1), uturn[:, low:high], 1, 0)
        turned = a * tab[1 - f, chunk, :, low:high]
        if f == 0:
            turned = -turned
        hi, lo = halves(turned)
        n = nmat[:, pl.ds(pl.multiple_of(q * 512 + chunk * 128, 128), 128)].astype(BF16)
        cgrad[:, low:high] += dot(
            jnp.concatenate([n, n], axis=1), jnp.concatenate([hi, lo], axis=0), 1, 0
        )

    for f in range(2):
        back(f, place[f], 0, 256)
    for off in rounds:
        for f in range(2):
            for off2 in (0, 1, 3, 2):
                waits1[f, off, off2].wait_recv()
            chunk = before(place[f], off, 4)
            if off == 2 and f == 1:
                back(f, chunk, 128, 256)
                xout[0:128, :] = fgrad[128:256, :]
                xout[128:144, :] = cgrad[:, 128:256]
                wait_mate = send(xout, xin, xin, partner)
                back(f, chunk, 0, 128)
            else:
                back(f, chunk, 0, 256)
    fown = fgrad[0:128, :] + gshort[...]
    wait_mate.wait_recv()

    du = (fown + xin[0:128, :]) * dsilu[...]
    daggregate = dot(du, wmix[...], 1, 1, HIGH)
    basis[...] = dot(w2[...], daggregate, 1, 1, HIGH)

    def radial_back(r, carry):
        rate, grad = carry
        d = basis[pl.ds(pl.multiple_of(r * 8, 8), 8), :] * (-2.0 * rate)
        k = kinds[...]
        chosen = jnp.zeros((SLOTS, 128), F32)
        for s in range(SPECIES):
            chosen = jnp.where(k == s, d[s : s + 1, :], chosen)
        return rate * GROWTH, grad + chosen * expo[r]

    _, slope = lax.fori_loop(
        0, BASIS, radial_back, (jnp.float32(RATE), jnp.zeros((SLOTS, 128), F32))
    )
    spent = []
    for d in range(3):
        g = slope * vec[d]
        vgrad[d] = g
        spent.append(jnp.sum(g, axis=0, keepdims=True))
    for a in range(3):
        for b in range(a, 3):
            s = jnp.sum(vgrad[a] * vec[b], axis=0, keepdims=True)
            s = jnp.sum(s, axis=1, keepdims=True)
            there = (rows8 == a) & (lanes8 == b)
            if a != b:
                there = there | ((rows8 == b) & (lanes8 == a))
            tile = tile - jnp.where(there, s, 0.0)

    def gather(buffer, value, me, to):
        buffer[me] = value
        return [
            send(buffer.at[me], buffer.at[me], buffer.at[before(me, off, 16)], to(off))
            for off in (8, 7, 9, 6, 10, 5, 11, 4, 12, 3, 13, 2, 14, 1, 15)
        ]

    def add_up(buffer):
        value = buffer[0]
        for i in range(1, 16):
            value = value + buffer[i]
        return value

    waits_v = gather(va, tile, m_zq, among_zq)

    rows16 = iota((16, 128), 0)

    def scatter(g, total):
        left = []
        for s in range(4):
            at = pl.ds(g * 4 + s, 1)
            page = lax.shift_right_logical(nbr[0, 0, at, :], 7)
            lines = jnp.concatenate(
                [jnp.where(rows16 == page, vgrad[d, at, :], 0.0) for d in range(3)], axis=0
            )
            left.append(jnp.concatenate(halves(lines), axis=0))
        return total + dot(jnp.concatenate(left, axis=1), marks[g], 1, 1)

    total = lax.fori_loop(0, SLOTS // 4, scatter, jnp.zeros((96, 128), F32))
    tgrad[...] = total[0:48, :] + total[48:96, :]
    for p in range(8):
        for d in range(3):
            gback[p, d : d + 1, :] = tgrad[16 * d + p + 1 : 16 * d + p + 2, :]
    waits_g = [send(gback.at[p], gret.at[7 - p], gret.at[7 - p], ghosts[p]) for p in range(8)]

    for w in waits_v:
        w.wait_recv()
    waits_v = gather(vb, add_up(va), m_xy, among_xy)
    for w in waits_g:
        w.wait_recv()
    left = []
    for d in range(8):
        hi, lo = halves(jnp.concatenate([gret[d], jnp.zeros((8, 128), F32)], axis=0))
        left.append(jnp.concatenate([hi, lo], axis=0))
    back_home = dot(jnp.concatenate(left, axis=1), gmarks[...], 1, 1)
    back_home = back_home[0:16, :] + back_home[16:32, :]
    moved = cgrad[:, 0:128] + xin[128:144, :]
    for d in range(3):
        grad = (
            tgrad[16 * d : 16 * d + 1, :]
            - spent[d]
            + moved[d : d + 1, :] * (2.0 * math.pi / LENGTHS[d])
            + back_home[d : d + 1, :]
        )
        out[d : d + 1, :] = -grad
    for w in waits_v:
        w.wait_recv()
    out[4:7, :] = (add_up(vb) * (1.0 / VOLUME))[0:3, :]
    for copy in started:
        copy.wait_send()


def per_device(
    positions, species, counts, neighbours, ghost_index, wave_numbers, embedding,
    w_radial, w_mix, w_read, w_out, amplitude, kernel_width, filter_gain,
):
    result = pl.pallas_call(
        kernel,
        out_shape=jax.ShapeDtypeStruct((8, 128), F32),
        in_specs=[pl.BlockSpec(memory_space=pltpu.HBM)] * 14,
        out_specs=pl.BlockSpec(memory_space=pltpu.VMEM),
        scratch_shapes=[pltpu.VMEM(shape, dtype) for shape, dtype in INPUTS]
        + [pltpu.VMEM(shape, dtype) for _, shape, dtype in SCRATCH]
        + [
            pltpu.SemaphoreType.DMA((N_COPIES,)),
            pltpu.SemaphoreType.DMA((N_COPIES,)),
            pltpu.SemaphoreType.DMA((14,)),
        ],
        compiler_params=pltpu.CompilerParams(collective_id=0, has_side_effects=True),
        name="ewald",
    )(
        positions, species, counts, neighbours, ghost_index, wave_numbers, embedding,
        w_radial, w_mix, w_read, w_out.reshape(1, 128), amplitude.reshape(1, 128),
        kernel_width.reshape(1, 128), filter_gain,
    )
    return result[0:3].reshape(3, 1, 1, 128), result[4:7, 0:3]


def solution(mesh):
    return jax.shard_map(
        per_device,
        mesh=mesh,
        in_specs=(
            P(None, "row", "col", None),
            P("row", "col", None),
            P("row", "col", None),
            P("row", "col", None, None),
            P("row", "col", None, None),
            P(), P(), P(), P(), P(), P(), P(), P(), P(),
        ),
        out_specs=(P(None, "row", "col", None), P()),
        check_vma=False,
    )
```

```python
import functools
import math

import jax
import jax.numpy as jnp
from jax import lax
from jax.experimental import pallas as pl
from jax.experimental.pallas import tpu as pltpu
from jax.sharding import PartitionSpec as P

CELL_EDGE = 12.0
HEIGHT = 36.0
ROWS = 32
COLS = 8
VOLUME = CELL_EDGE * ROWS * CELL_EDGE * COLS * HEIGHT
LENGTHS = (CELL_EDGE * ROWS, CELL_EDGE * COLS, HEIGHT)
DIRECTIONS = ((-1, -1), (-1, 0), (-1, 1), (0, -1), (0, 1), (1, -1), (1, 0), (1, 1))
RATE = 0.003
GROWTH = 1.6
BASIS = 16
SPECIES = 6
SLOTS = 64
WAVES = 1000
HIGH = lax.Precision.HIGH
HIGHEST = lax.Precision.HIGHEST
MESH = pl.DeviceIdType.MESH
F32 = jnp.float32
BF16 = jnp.bfloat16
SINE = (
    6.2831854820251465,
    -41.34170150756836,
    81.60513305664062,
    -76.70301818847656,
    42.02592849731445,
    -14.899847030639648,
    3.2381374835968018,
)
COSINE = (
    1.0,
    -19.73920440673828,
    64.93911743164062,
    -85.45014190673828,
    60.16762924194336,
    -25.967599868774414,
    6.528658390045166,
)
def dot(a, b, ca, cb, precision=None):
    return lax.dot_general(
        a, b, (((ca,), (cb,)), ((), ())), precision=precision, preferred_element_type=F32
    )


def horner(coefs, w):
    value = jnp.full_like(w, coefs[-1])
    for c in coefs[-2::-1]:
        value = value * w + c
    return value


def halves(x):
    hi = x.astype(BF16)
    lo = (x - hi.astype(F32)).astype(BF16)
    return hi, lo


def iota(shape, dim):
    return lax.broadcasted_iota(jnp.int32, shape, dim)


N_COPIES = 132
FAR_FIRST = (8, 7, 9, 6, 10, 5, 11, 4, 12, 3, 13, 2, 14, 1, 15)
PAIRS = ((0, 0), (0, 1), (0, 2), (1, 1), (1, 2), (2, 2))
INPUTS = (
    ((3, 1, 1, 128), F32), ((1, 1, 128), jnp.int32), ((1, 1, 128), jnp.int32),
    ((1, 1, 64, 128), jnp.int32), ((1, 1, 8, 128), jnp.int32), ((3, 1000), jnp.int32),
    ((6, 128), F32), ((16, 128), F32), ((128, 128), F32), ((128, 128), F32), ((1, 128), F32),
    ((1, 128), F32), ((1, 128), F32), ((1000, 128), F32),
)
SCRATCH = (
    ("own", (8, 128), F32), ("mate", (8, 128), F32), ("gsend", (8, 8, 128), F32),
    ("pages", (9, 8, 128), F32), ("gback", (8, 8, 128), F32), ("gret", (8, 8, 128), F32),
    ("nmat", (16, 1024), F32), ("umat", (16, 256), F32), ("tab", (2, 4, 128, 256), F32),
    ("tsplit", (2, 4, 128, 768), BF16), ("tturn", (2, 4, 256, 384), BF16),
    ("emb8", (8, 128), F32), ("w2", (128, 128), F32),
    ("vec", (3, 64, 128), F32), ("kinds", (64, 128), F32), ("dist", (64, 128), F32),
    ("expo", (16, 64, 128), F32), ("basis", (128, 128), F32), ("upd", (256, 128), F32),
    ("usplit", (768, 128), BF16), ("uturn", (384, 256), BF16),
    ("dsilu", (128, 128), F32), ("gshort", (128, 128), F32),
    ("sums", (2, 4, 4, 32, 128), F32), ("in1", (2, 3, 4, 32, 128), F32),
    ("part", (2, 4, 32, 128), F32), ("in2", (2, 3, 32, 128), F32),
    ("zin", (7, 8, 128), F32), ("zbuf", (64, 128), F32), ("c3", (64, 128), F32),
    ("coef", (2, 4, 4, 32, 128), F32), ("fgrad", (256, 128), F32), ("cgrad", (16, 256), F32),
    ("xout", (144, 128), F32), ("xin", (144, 128), F32),
    ("marks", (16, 128, 512), BF16), ("gmarks", (128, 1024), BF16),
    ("vgrad", (3, 64, 128), F32), ("tgrad", (48, 128), F32),
    ("pair", (6, 64, 128), F32), ("moment", (6, 128, 128), F32),
    ("uvir", (2, 6, 128, 128), F32),
    ("va", (16, 8, 128), F32), ("vb", (16, 8, 128), F32),
)


def kernel(*refs):
    ins, out = refs[:14], refs[14]
    here = refs[15:29]
    named = refs[29 : 29 + len(SCRATCH)]
    ssem, rsem, lsem = refs[29 + len(SCRATCH) :]
    (pos, spec, cnt, nbr, gidx, wn, emb, wrad, wmix, wread, wout, amp, width, gain) = here
    (
        own, mate, gsend, pages, gback, gret, nmat, umat, tab, tsplit, tturn, emb8, w2,
        vec, kinds, dist, expo, basis, upd, usplit, uturn, dsilu, gshort,
        sums, in1, part, in2, zin, zbuf, c3, coef, fgrad, cgrad, xout, xin,
        marks, gmarks, vgrad, tgrad, pair, moment, uvir, va, vb,
    ) = named
    row = lax.axis_index("row")
    col = lax.axis_index("col")
    q = lax.rem(row, 2)
    zl = lax.rem(lax.div(row, 2), 4)
    y = lax.div(row, 8)
    x = lax.rem(col, 4)
    zh = lax.div(col, 4)
    z = zh * 4 + zl

    def device(q, x, y, z):
        return (y * 8 + lax.rem(z, 4) * 2 + q, lax.div(z, 4) * 4 + x)

    ghosts = [
        (lax.rem(row + a + ROWS, ROWS), lax.rem(col + b + COLS, COLS)) for a, b in DIRECTIONS
    ]
    partner = device(1 - q, x, y, z)

    def along_x(off):
        return device(q, lax.rem(x + off, 4), y, z)

    def along_y(off):
        return device(q, x, lax.rem(y + off, 4), z)

    def along_z(off):
        return device(q, x, y, lax.rem(z + off, 8))

    m_zq = z * 2 + q
    m_xy = x * 4 + y

    def among_zq(off):
        m = lax.rem(m_zq + off, 16)
        return device(lax.rem(m, 2), x, y, lax.div(m, 2))

    def among_xy(off):
        m = lax.rem(m_xy + off, 16)
        return device(q, lax.div(m, 4), lax.rem(m, 4), z)

    def before(i, off, n):
        return lax.rem(i + n - off, n)

    def after(i, off, n):
        return lax.rem(i + off, n)

    loads = [pltpu.make_async_copy(ins[i], here[i], lsem.at[i]) for i in range(14)]
    for copy in loads:
        copy.start()
    barrier = pltpu.get_barrier_semaphore()
    greeted = (
        ghosts
        + [among_zq(off) for off in FAR_FIRST]
        + [among_xy(off) for off in FAR_FIRST]
    )
    for who in greeted:
        pl.semaphore_signal(barrier, inc=1, device_id=who, device_id_type=MESH)

    started = []

    def send(src, dst, landing, who):
        i = len(started)
        copy = pltpu.make_async_remote_copy(
            src_ref=src,
            dst_ref=dst,
            send_sem=ssem.at[i],
            recv_sem=rsem.at[i],
            device_id=who,
            device_id_type=MESH,
        )
        copy.start()
        started.append(copy)
        return pltpu.make_async_remote_copy(
            src_ref=src,
            dst_ref=landing,
            send_sem=ssem.at[i],
            recv_sem=rsem.at[i],
            device_id=who,
            device_id_type=MESH,
        )

    gback[...] = jnp.zeros((8, 8, 128), F32)
    nmat[...] = jnp.zeros((16, 1024), F32)
    umat[...] = jnp.zeros((16, 256), F32)
    emb8[...] = jnp.zeros((8, 128), F32)
    own[...] = jnp.zeros((8, 128), F32)
    for copy in loads:
        copy.wait()

    for d in range(3):
        own[d : d + 1, :] = pos[d, 0]
    own[3:4, :] = spec[0].astype(F32)
    table = own[...]
    for d in range(8):
        index = jnp.broadcast_to(gidx[0, 0, d : d + 1, :], (8, 128))
        gsend[d] = jnp.take_along_axis(table, index, axis=1, mode="promise_in_bounds")
    pages[0] = table
    numbers = wn[...].astype(F32)
    for p in range(3):
        nmat[3 * p : 3 * p + 3, 0:WAVES] = numbers

    pl.semaphore_wait(barrier, len(greeted))
    wait_mate = send(own, mate, mate, partner)
    waits = [
        send(gsend.at[d], pages.at[8 - d], pages.at[8 - d], ghosts[d]) for d in range(8)
    ]

    emb8[0:SPECIES, :] = emb[...]
    kinds8 = emb8[...]
    for r in range(BASIS):
        w2[8 * r : 8 * r + 8, :] = wrad[r : r + 1, :] * kinds8 * (1.0 / SLOTS)
    onehot = (spec[0] == iota((8, 128), 0)).astype(F32)
    start = dot(onehot, kinds8, 0, 0, HIGHEST)

    wait_mate.wait_recv()
    column = col.astype(F32) * CELL_EDGE
    offsets = (
        (row.astype(F32) * CELL_EDGE, column, 0.0),
        ((row + 1 - 2 * q).astype(F32) * CELL_EDGE, column, 0.0),
    )
    for side, ref in enumerate((own, mate)):
        for d in range(3):
            turn = (ref[d : d + 1, :] + offsets[side][d]) * (1.0 / LENGTHS[d])
            for p in range(3):
                piece = turn.astype(BF16).astype(F32)
                umat[3 * p + d : 3 * p + d + 1, 128 * side : 128 * side + 128] = piece
                turn = turn - piece
    fractions = umat[...].astype(BF16)

    def trig(i, carry):
        block = nmat[:, pl.ds(pl.multiple_of(q * 512 + i * 128, 128), 128)].astype(BF16)
        turns = dot(block, fractions, 0, 0)
        turns = turns - jnp.floor(turns + 0.5)
        w = turns * turns
        for f, value in enumerate((horner(COSINE, w), horner(SINE, w) * turns)):
            tab[f, i] = value
            hi, lo = halves(value)
            for side in range(2):
                mine = slice(128 * side, 128 * side + 128)
                for p, half in enumerate((hi, lo, hi)):
                    at = 384 * side + 128 * p
                    tsplit[f, i, :, at : at + 128] = half[:, mine]
        turns = dot(fractions, block, 0, 0)
        turns = turns - jnp.floor(turns + 0.5)
        w = turns * turns
        for f, value in enumerate((horner(COSINE, w), horner(SINE, w) * turns)):
            hi, lo = halves(value)
            for p, half in enumerate((hi, lo, hi)):
                tturn[f, i, :, 128 * p : 128 * p + 128] = half
        return carry

    lax.fori_loop(0, 4, trig, 0)

    for w in waits:
        w.wait_recv()
    live = cnt[0]
    rows8 = iota((8, 128), 0)

    def edge(g, carry):
        at = pl.multiple_of(g * 8, 8)
        index = nbr[0, 0, pl.ds(at, 8), :]
        page = lax.shift_right_logical(index, 7)
        lane = lax.bitwise_and(index, 127)
        picked = [jnp.zeros((8, 128), F32)] * 4
        for p in range(9):
            here = page == p
            for d in range(4):
                line = pages[p, d : d + 1, :]
                if p > 0 and d < 2 and DIRECTIONS[p - 1][d]:
                    line = line + CELL_EDGE * DIRECTIONS[p - 1][d]
                found = jnp.take_along_axis(
                    jnp.broadcast_to(line, (8, 128)), lane, axis=1, mode="promise_in_bounds"
                )
                picked[d] = jnp.where(here, found, picked[d])
        square = jnp.zeros((8, 128), F32)
        for d in range(3):
            v = picked[d] - pos[d, 0]
            vec[d, pl.ds(at, 8), :] = v
            square = square + v * v
        dist[pl.ds(at, 8), :] = square
        kinds[pl.ds(at, 8), :] = jnp.where(rows8 + at < live, picked[3], -1.0)
        return carry

    lax.fori_loop(0, 8, edge, 0, unroll=2)

    def radial(r, rate):
        e = jnp.exp(dist[...] * (-rate))
        expo[r] = e
        k = kinds[...]
        tile = jnp.zeros((8, 128), F32)
        for s in range(SPECIES):
            total = jnp.sum(jnp.where(k == s, e, 0.0), axis=0, keepdims=True)
            tile = jnp.where(rows8 == s, total, tile)
        basis[pl.ds(pl.multiple_of(r * 8, 8), 8), :] = tile
        return rate * GROWTH

    lax.fori_loop(0, BASIS, radial, jnp.float32(RATE), unroll=4)

    aggregate = dot(basis[...], w2[...], 0, 0, HIGH)
    u = dot(aggregate, wmix[...], 1, 0, HIGH)
    gate = 1.0 / (1.0 + jnp.exp(-u))
    mine = start + u * gate
    upd[0:128, :] = mine
    wait_mate = send(upd.at[0:128], upd.at[128:256], upd.at[128:256], partner)
    dsilu[...] = gate * (1.0 + u * (1.0 - gate))
    p = dot(mine, wread[...], 1, 0, HIGH)
    gate = 1.0 / (1.0 + jnp.exp(-p))
    gshort[...] = dot(wout[...] * (gate * (1.0 + p * (1.0 - gate))), wread[...], 1, 1, HIGH)

    def split(side):
        value = upd[128 * side : 128 * side + 128, :]
        hi, lo = halves(value)
        for p, half in enumerate((hi, hi, lo)):
            usplit[384 * side + 128 * p : 384 * side + 128 * p + 128, :] = half

    def split_turned(side):
        hi, lo = halves(upd[128 * side : 128 * side + 128, :].T)
        for p, half in enumerate((hi, hi, lo)):
            uturn[128 * p : 128 * p + 128, 128 * side : 128 * side + 128] = half

    split(0)
    wait_mate.wait_recv()
    split(1)

    place = (x, y)
    second = (y, x)
    along = (along_x, along_y)
    order = (2, 1, 3, 0)
    waits1 = {}
    for off in order:
        for f in range(2):
            chunk = after(place[f], off, 4)
            value = dot(tsplit[f, chunk], usplit[...], 1, 0)
            sums[f, chunk] = value.reshape(4, 32, 128)
            if off == 0:
                continue
            for off2 in order:
                waits1[f, off, off2] = send(
                    sums.at[f, chunk, after(second[f], off2, 4)],
                    in1.at[f, off - 1, off2],
                    in1.at[f, off - 1, off2],
                    along[f](off),
                )
    waits2 = {}
    for off2 in order:
        for f in range(2):
            for off in (1, 3, 2):
                waits1[f, off, off2].wait_recv()
            total = (
                sums[f, place[f], after(second[f], off2, 4)]
                + in1[f, 0, off2]
                + in1[f, 1, off2]
                + in1[f, 2, off2]
            )
            if off2 == 0:
                zbuf[32 * f : 32 * f + 32, :] = total
                continue
            part[f, off2] = total
            waits2[f, off2] = send(
                part.at[f, off2], in2.at[f, off2 - 1], in2.at[f, off2 - 1], along[1 - f](off2)
            )
    for f in range(2):
        for off2 in (1, 3, 2):
            waits2[f, off2].wait_recv()
        zbuf[32 * f : 32 * f + 32, :] += in2[f, 0] + in2[f, 1] + in2[f, 2]
    waits = []
    for off in (4, 3, 5, 2, 6, 1, 7):
        at = pl.ds(pl.multiple_of(after(z, off, 8) * 8, 8), 8)
        waits.append(send(zbuf.at[at], zin.at[off - 1], zin.at[off - 1], along_z(off)))

    first = 512 * q + (1 - zh) * (128 * x + 32 * y) + zh * (128 * y + 32 * x) + 8 * zl
    chosen = (iota((8, 1024), 1) == iota((8, 1024), 0) + first).astype(BF16)
    mine = dot(chosen, nmat[...].astype(BF16), 1, 1)
    k_of = [mine[:, d : d + 1] * (2.0 * math.pi / LENGTHS[d]) for d in range(3)]
    norm = k_of[0] * k_of[0] + k_of[1] * k_of[1] + k_of[2] * k_of[2]
    inside = lax.div(first, WAVES)
    source = pl.multiple_of(first - inside * WAVES, 8)
    weight = amp[...] * gain[pl.ds(source, 8), :] * jnp.exp(-width[...] * norm)
    weight = jnp.where(rows8 + first < WAVES, weight * (1.0 / VOLUME), 0.0)

    rows128 = iota((128, 128), 0)

    def mark(g, carry):
        for s in range(4):
            lane = lax.bitwise_and(nbr[0, 0, pl.ds(g * 4 + s, 1), :], 127)
            marks[g, :, 128 * s : 128 * s + 128] = (rows128 == lane).astype(F32).astype(BF16)
        return carry

    lax.fori_loop(0, 16, mark, 0)
    for d in range(8):
        gmarks[:, 128 * d : 128 * d + 128] = (
            (rows128 == gidx[0, 0, d : d + 1, :]).astype(F32).astype(BF16)
        )

    split_turned(0)
    split_turned(1)
    for m, (a, b) in enumerate(PAIRS):
        pair[m] = vec[a] * vec[b]

    def moments(r, rate):
        e = expo[r] * (2.0 * rate)
        k = kinds[...]
        parts = [jnp.where(k == s, e, 0.0) for s in range(SPECIES)]
        for m in range(6):
            v = pair[m]
            tile = jnp.zeros((8, 128), F32)
            for s in range(SPECIES):
                total = jnp.sum(parts[s] * v, axis=0, keepdims=True)
                tile = jnp.where(rows8 == s, total, tile)
            moment[m, pl.ds(pl.multiple_of(r * 8, 8), 8), :] = tile
        return rate * GROWTH

    lax.fori_loop(0, BASIS, moments, jnp.float32(RATE))

    for w in waits:
        w.wait_recv()
    total = zbuf[pl.ds(pl.multiple_of(z * 8, 8), 8), :]
    for i in range(7):
        total = total + zin[i]
    result = weight * total
    mine_z = pl.ds(pl.multiple_of(z * 8, 8), 8)
    c3[mine_z, :] = result
    waits = []
    for off in (4, 3, 5, 2, 6, 1, 7):
        at = pl.ds(pl.multiple_of(before(z, off, 8) * 8, 8), 8)
        waits.append(send(c3.at[mine_z], c3.at[mine_z], c3.at[at], along_z(off)))

    power = result * total
    strain = jnp.sum(width[...] * power, axis=1, keepdims=True)
    energy = 0.5 * jnp.sum(jnp.sum(power, axis=1, keepdims=True), axis=0, keepdims=True)
    lanes8 = iota((8, 128), 1)
    tile = jnp.where((rows8 == lanes8) & (rows8 < 3), energy, 0.0)
    for a in range(3):
        for b in range(a, 3):
            s = jnp.sum(k_of[a] * k_of[b] * strain, axis=0, keepdims=True)
            there = (rows8 == a) & (lanes8 == b)
            if a != b:
                there = there | ((rows8 == b) & (lanes8 == a))
            tile = tile - jnp.where(there, s, 0.0)

    for m in range(6):
        answer = dot(moment[m], w2[...], 0, 0, HIGH)
        uvir[0, m] = dot(answer, wmix[...], 1, 0, HIGH) * dsilu[...]
    wait_uvir = send(uvir.at[0], uvir.at[1], uvir.at[1], partner)
    fgrad[...] = jnp.zeros((256, 128), F32)
    cgrad[...] = jnp.zeros((16, 256), F32)

    for w in waits:
        w.wait_recv()

    rounds = (1, 3, 2)
    waits2, waits1 = {}, {}

    def spread(f, off2, piece, src):
        for off in (2, 1, 3):
            waits1[f, off, off2] = send(
                src,
                coef.at[f, place[f], piece],
                coef.at[f, before(place[f], off, 4), piece],
                along[f](off),
            )

    for off2 in (2, 1, 3):
        for f in range(2):
            waits2[f, off2] = send(
                c3.at[32 * f : 32 * f + 32],
                coef.at[f, place[f], second[f]],
                coef.at[f, place[f], before(second[f], off2, 4)],
                along[1 - f](off2),
            )
    for f in range(2):
        spread(f, 0, second[f], c3.at[32 * f : 32 * f + 32])
        coef[f, place[f], second[f]] = c3[32 * f : 32 * f + 32, :]
    for off2 in rounds:
        for f in range(2):
            waits2[f, off2].wait_recv()
            piece = before(second[f], off2, 4)
            spread(f, off2, piece, coef.at[f, place[f], piece])

    def back(f, chunk, low, high):
        c = coef[f, chunk].reshape(128, 128)
        hi, lo = halves(c)
        fgrad[low:high, :] += dot(
            tturn[f, chunk, low:high, :], jnp.concatenate([hi, hi, lo], axis=0), 1, 0
        )
        a = dot(jnp.concatenate([hi, lo, hi], axis=1), uturn[:, low:high], 1, 0)
        turned = a * tab[1 - f, chunk, :, low:high]
        if f == 0:
            turned = -turned
        hi, lo = halves(turned)
        n = nmat[:, pl.ds(pl.multiple_of(q * 512 + chunk * 128, 128), 128)].astype(BF16)
        cgrad[:, low:high] += dot(
            jnp.concatenate([n, n], axis=1), jnp.concatenate([hi, lo], axis=0), 1, 0
        )

    for f in range(2):
        back(f, place[f], 0, 256)
    for off in rounds:
        for f in range(2):
            for off2 in (0, 1, 3, 2):
                waits1[f, off, off2].wait_recv()
            chunk = before(place[f], off, 4)
            if off == 2 and f == 1:
                back(f, chunk, 128, 256)
                xout[0:128, :] = fgrad[128:256, :]
                xout[128:144, :] = cgrad[:, 128:256]
                wait_mate = send(xout, xin, xin, partner)
                back(f, chunk, 0, 128)
            else:
                back(f, chunk, 0, 256)
    def gather(buffer, value, me, to):
        buffer[me] = value
        return [
            send(buffer.at[me], buffer.at[me], buffer.at[before(me, off, 16)], to(off))
            for off in FAR_FIRST
        ]

    def add_up(buffer):
        value = buffer[0]
        for i in range(1, 16):
            value = value + buffer[i]
        return value

    fown = fgrad[0:128, :] + gshort[...]
    wait_uvir.wait_recv()
    for m, (a, b) in enumerate(PAIRS):
        s = jnp.sum(fown * uvir[0, m] + fgrad[128:256, :] * uvir[1, m], axis=0, keepdims=True)
        s = jnp.sum(s, axis=1, keepdims=True)
        there = (rows8 == a) & (lanes8 == b)
        if a != b:
            there = there | ((rows8 == b) & (lanes8 == a))
        tile = tile + jnp.where(there, s, 0.0)
    waits_v = gather(va, tile, m_zq, among_zq)
    wait_mate.wait_recv()

    du = (fown + xin[0:128, :]) * dsilu[...]
    daggregate = dot(du, wmix[...], 1, 1, HIGH)
    basis[...] = dot(w2[...], daggregate, 1, 1, HIGH)

    def radial_back(r, carry):
        rate, grad = carry
        d = basis[pl.ds(pl.multiple_of(r * 8, 8), 8), :] * (-2.0 * rate)
        k = kinds[...]
        chosen = jnp.zeros((SLOTS, 128), F32)
        for s in range(SPECIES):
            chosen = jnp.where(k == s, d[s : s + 1, :], chosen)
        return rate * GROWTH, grad + chosen * expo[r]

    _, slope = lax.fori_loop(
        0, BASIS, radial_back, (jnp.float32(RATE), jnp.zeros((SLOTS, 128), F32)), unroll=4
    )
    spent = []
    for d in range(3):
        g = slope * vec[d]
        vgrad[d] = g
        spent.append(jnp.sum(g, axis=0, keepdims=True))

    rows16 = iota((16, 128), 0)

    def scatter(g, total):
        left = []
        for s in range(4):
            at = pl.ds(g * 4 + s, 1)
            page = lax.shift_right_logical(nbr[0, 0, at, :], 7)
            lines = jnp.concatenate(
                [jnp.where(rows16 == page, vgrad[d, at, :], 0.0) for d in range(3)], axis=0
            )
            left.append(jnp.concatenate(halves(lines), axis=0))
        return total + dot(jnp.concatenate(left, axis=1), marks[g], 1, 1)

    total = lax.fori_loop(0, SLOTS // 4, scatter, jnp.zeros((96, 128), F32), unroll=2)
    tgrad[...] = total[0:48, :] + total[48:96, :]
    for p in range(8):
        for d in range(3):
            gback[p, d : d + 1, :] = tgrad[16 * d + p + 1 : 16 * d + p + 2, :]
    waits_g = [send(gback.at[p], gret.at[7 - p], gret.at[7 - p], ghosts[p]) for p in range(8)]

    for w in waits_v:
        w.wait_recv()
    waits_v = gather(vb, add_up(va), m_xy, among_xy)
    for w in waits_g:
        w.wait_recv()
    left = []
    for d in range(8):
        hi, lo = halves(jnp.concatenate([gret[d], jnp.zeros((8, 128), F32)], axis=0))
        left.append(jnp.concatenate([hi, lo], axis=0))
    back_home = dot(jnp.concatenate(left, axis=1), gmarks[...], 1, 1)
    back_home = back_home[0:16, :] + back_home[16:32, :]
    moved = cgrad[:, 0:128] + xin[128:144, :]
    for d in range(3):
        grad = (
            tgrad[16 * d : 16 * d + 1, :]
            - spent[d]
            + moved[d : d + 1, :] * (2.0 * math.pi / LENGTHS[d])
            + back_home[d : d + 1, :]
        )
        out[d : d + 1, :] = -grad
    for w in waits_v:
        w.wait_recv()
    out[4:7, :] = (add_up(vb) * (1.0 / VOLUME))[0:3, :]
    for copy in started:
        copy.wait_send()


def hand_over(result, force, virial):
    for d in range(3):
        force[d, 0] = result[d : d + 1, :]
    virial[...] = result[4:7, 0:3]


def per_device(
    positions, species, counts, neighbours, ghost_index, wave_numbers, embedding,
    w_radial, w_mix, w_read, w_out, amplitude, kernel_width, filter_gain,
):
    result = pl.pallas_call(
        kernel,
        out_shape=jax.ShapeDtypeStruct((8, 128), F32),
        in_specs=[pl.BlockSpec(memory_space=pltpu.HBM)] * 14,
        out_specs=pl.BlockSpec(memory_space=pltpu.VMEM),
        scratch_shapes=[pltpu.VMEM(shape, dtype) for shape, dtype in INPUTS]
        + [pltpu.VMEM(shape, dtype) for _, shape, dtype in SCRATCH]
        + [
            pltpu.SemaphoreType.DMA((N_COPIES,)),
            pltpu.SemaphoreType.DMA((N_COPIES,)),
            pltpu.SemaphoreType.DMA((14,)),
        ],
        compiler_params=pltpu.CompilerParams(collective_id=0, has_side_effects=True),
        name="ewald",
    )(
        positions, species, counts, neighbours, ghost_index, wave_numbers, embedding,
        w_radial, w_mix, w_read, w_out.reshape(1, 128), amplitude.reshape(1, 128),
        kernel_width.reshape(1, 128), filter_gain,
    )
    return pl.pallas_call(
        hand_over,
        out_shape=(
            jax.ShapeDtypeStruct((3, 1, 1, 128), F32),
            jax.ShapeDtypeStruct((3, 3), F32),
        ),
        in_specs=[pl.BlockSpec(memory_space=pltpu.VMEM)],
        out_specs=(
            pl.BlockSpec(memory_space=pltpu.VMEM),
            pl.BlockSpec(memory_space=pltpu.VMEM),
        ),
        name="hand_over",
    )(result)


def solution(mesh):
    return jax.shard_map(
        per_device,
        mesh=mesh,
        in_specs=(
            P(None, "row", "col", None),
            P("row", "col", None),
            P("row", "col", None),
            P("row", "col", None, None),
            P("row", "col", None, None),
            P(), P(), P(), P(), P(), P(), P(), P(), P(),
        ),
        out_specs=(P(None, "row", "col", None), P()),
        check_vma=False,
    )
```

```python
import functools
import math

import jax
import jax.numpy as jnp
from jax import lax
from jax.experimental import pallas as pl
from jax.experimental.pallas import tpu as pltpu
from jax.sharding import PartitionSpec as P

CELL_EDGE = 12.0
HEIGHT = 36.0
ROWS = 32
COLS = 8
VOLUME = CELL_EDGE * ROWS * CELL_EDGE * COLS * HEIGHT
LENGTHS = (CELL_EDGE * ROWS, CELL_EDGE * COLS, HEIGHT)
DIRECTIONS = ((-1, -1), (-1, 0), (-1, 1), (0, -1), (0, 1), (1, -1), (1, 0), (1, 1))
RATE = 0.003
GROWTH = 1.6
BASIS = 16
SPECIES = 6
SLOTS = 64
WAVES = 1000
HIGH = lax.Precision.HIGH
HIGHEST = lax.Precision.HIGHEST
MESH = pl.DeviceIdType.MESH
F32 = jnp.float32
BF16 = jnp.bfloat16
SINE = (
    6.2831854820251465,
    -41.34170150756836,
    81.60513305664062,
    -76.70301818847656,
    42.02592849731445,
    -14.899847030639648,
    3.2381374835968018,
)
COSINE = (
    1.0,
    -19.73920440673828,
    64.93911743164062,
    -85.45014190673828,
    60.16762924194336,
    -25.967599868774414,
    6.528658390045166,
)
def dot(a, b, ca, cb, precision=None):
    return lax.dot_general(
        a, b, (((ca,), (cb,)), ((), ())), precision=precision, preferred_element_type=F32
    )


def horner(coefs, w):
    value = jnp.full_like(w, coefs[-1])
    for c in coefs[-2::-1]:
        value = value * w + c
    return value


def halves(x):
    hi = x.astype(BF16)
    lo = (x - hi.astype(F32)).astype(BF16)
    return hi, lo


def iota(shape, dim):
    return lax.broadcasted_iota(jnp.int32, shape, dim)


N_COPIES = 132
FAR_ZQ = (9, 8, 7, 6, 11, 10, 5, 4, 13, 12, 3, 2, 15, 14, 1)
FAR_XY = (10, 9, 11, 6, 14, 5, 7, 13, 15, 8, 2, 4, 12, 1, 3)
PAIRS = ((0, 0), (0, 1), (0, 2), (1, 1), (1, 2), (2, 2))
INPUTS = (
    ((3, 1, 1, 128), F32), ((1, 1, 128), jnp.int32), ((1, 1, 128), jnp.int32),
    ((1, 1, 64, 128), jnp.int32), ((1, 1, 8, 128), jnp.int32), ((3, 1000), jnp.int32),
    ((6, 128), F32), ((16, 128), F32), ((128, 128), F32), ((128, 128), F32), ((1, 128), F32),
    ((1, 128), F32), ((1, 128), F32), ((1000, 128), F32),
)
SCRATCH = (
    ("own", (8, 128), F32), ("mate", (8, 128), F32), ("gsend", (8, 8, 128), F32),
    ("pages", (9, 8, 128), F32), ("gback", (8, 8, 128), F32), ("gret", (8, 8, 128), F32),
    ("nmat", (16, 1024), F32), ("umat", (16, 256), F32), ("tab", (2, 4, 4, 32, 256), F32),
    ("tsplit", (2, 4, 128, 768), BF16), ("thi", (2, 4, 4, 32, 256), BF16),
    ("tlo", (2, 4, 4, 32, 256), BF16), ("nb", (3, 4, 4, 32, 128), F32),
    ("emb8", (8, 128), F32), ("w2", (128, 128), F32),
    ("vec", (3, 64, 128), F32), ("kinds", (64, 128), F32), ("dist", (64, 128), F32),
    ("expo", (16, 64, 128), F32), ("basis", (128, 128), F32), ("upd", (256, 128), F32),
    ("usplit", (768, 128), BF16), ("uturn", (384, 256), BF16),
    ("dsilu", (128, 128), F32), ("gshort", (128, 128), F32),
    ("sums", (2, 4, 4, 32, 128), F32), ("in1", (2, 3, 4, 32, 128), F32),
    ("part", (2, 4, 32, 128), F32), ("in2", (2, 3, 32, 128), F32),
    ("zin", (7, 8, 128), F32), ("zbuf", (64, 128), F32), ("c3", (64, 128), F32),
    ("coef", (2, 4, 4, 32, 128), F32), ("fgrad", (128, 256), F32), ("cgrad", (3, 8, 256), F32),
    ("xout", (152, 128), F32), ("xin", (152, 128), F32),
    ("marks", (16, 128, 512), BF16), ("gmarks", (128, 1024), BF16),
    ("vgrad", (3, 64, 128), F32), ("tgrad", (48, 128), F32),
    ("pair", (6, 64, 128), F32), ("moment", (6, 128, 128), F32),
    ("uvir", (2, 6, 128, 128), F32),
    ("va", (16, 1, 128), F32), ("vb", (16, 1, 128), F32),
)


def kernel(*refs):
    ins, out = refs[:14], refs[14]
    here = refs[15:29]
    named = refs[29 : 29 + len(SCRATCH)]
    ssem, rsem, lsem = refs[29 + len(SCRATCH) :]
    (pos, spec, cnt, nbr, gidx, wn, emb, wrad, wmix, wread, wout, amp, width, gain) = here
    (
        own, mate, gsend, pages, gback, gret, nmat, umat, tab, tsplit, thi, tlo, nb, emb8, w2,
        vec, kinds, dist, expo, basis, upd, usplit, uturn, dsilu, gshort,
        sums, in1, part, in2, zin, zbuf, c3, coef, fgrad, cgrad, xout, xin,
        marks, gmarks, vgrad, tgrad, pair, moment, uvir, va, vb,
    ) = named
    row = lax.axis_index("row")
    col = lax.axis_index("col")
    q = lax.rem(row, 2)
    zl = lax.rem(lax.div(row, 2), 4)
    y = lax.div(row, 8)
    x = lax.rem(col, 4)
    zh = lax.div(col, 4)
    z = zh * 4 + zl

    xs = [x] + [lax.rem(x + off, 4) for off in (1, 2, 3)]
    ys = [y] + [lax.rem(y + off, 4) for off in (1, 2, 3)]
    zs = [z] + [lax.rem(z + off, 8) for off in range(1, 8)]
    z_cols = [lax.div(at, 4) * 4 for at in zs]
    z_rows = [(at - high) * 2 for at, high in zip(zs, z_cols)]
    y_rows = [at * 8 for at in ys]
    cores = [q, 1 - q]
    x_base = z_cols[0]
    y_base = z_rows[0] + q

    up, down = lax.rem(row + 1, ROWS), lax.rem(row + ROWS - 1, ROWS)
    east, west = lax.rem(col + 1, COLS), lax.rem(col + COLS - 1, COLS)
    ghosts = [((down, row, up)[a + 1], (west, col, east)[b + 1]) for a, b in DIRECTIONS]
    partner = (row + 1 - 2 * q, col)

    def along_x(off):
        return (row, x_base + xs[off])

    def along_y(off):
        return (y_rows[off] + y_base, col)

    def along_z(off):
        return (y_rows[0] + z_rows[off] + q, z_cols[off] + x)

    def among_zq(off):
        dz, dq = off // 2, off % 2
        return (y_rows[0] + z_rows[dz] + cores[dq], z_cols[dz] + x)

    def among_xy(off):
        dx, dy = off // 4, off % 4
        return (y_rows[dy] + y_base, x_base + xs[dx])

    m_zq = z * 2 + q
    m_xy = x * 4 + y

    def from_zq(off):
        dz, dq = off // 2, off % 2
        return zs[(8 - dz) % 8] * 2 + cores[dq]

    def from_xy(off):
        dx, dy = off // 4, off % 4
        return xs[(4 - dx) % 4] * 4 + ys[(4 - dy) % 4]

    loads = [pltpu.make_async_copy(ins[i], here[i], lsem.at[i]) for i in range(14)]
    for copy in loads:
        copy.start()
    barrier = pltpu.get_barrier_semaphore()
    greeted = (
        ghosts + [among_zq(off) for off in FAR_ZQ] + [among_xy(off) for off in FAR_XY]
    )
    for who in greeted:
        pl.semaphore_signal(barrier, inc=1, device_id=who, device_id_type=MESH)

    started = []

    def send(src, dst, landing, who):
        i = len(started)
        copy = pltpu.make_async_remote_copy(
            src_ref=src,
            dst_ref=dst,
            send_sem=ssem.at[i],
            recv_sem=rsem.at[i],
            device_id=who,
            device_id_type=MESH,
        )
        copy.start()
        started.append(copy)
        return pltpu.make_async_remote_copy(
            src_ref=src,
            dst_ref=landing,
            send_sem=ssem.at[i],
            recv_sem=rsem.at[i],
            device_id=who,
            device_id_type=MESH,
        )

    gback[...] = jnp.zeros((8, 8, 128), F32)
    nmat[...] = jnp.zeros((16, 1024), F32)
    umat[...] = jnp.zeros((16, 256), F32)
    emb8[...] = jnp.zeros((8, 128), F32)
    own[...] = jnp.zeros((8, 128), F32)
    for copy in loads:
        copy.wait()

    for d in range(3):
        own[d : d + 1, :] = pos[d, 0]
    own[3:4, :] = spec[0].astype(F32)
    table = own[...]
    for d in range(8):
        index = jnp.broadcast_to(gidx[0, 0, d : d + 1, :], (8, 128))
        gsend[d] = jnp.take_along_axis(table, index, axis=1, mode="promise_in_bounds")
    pages[0] = table
    numbers = wn[...].astype(F32)
    for p in range(3):
        nmat[3 * p : 3 * p + 3, 0:WAVES] = numbers

    pl.semaphore_wait(barrier, len(greeted))
    wait_mate = send(own, mate, mate, partner)
    waits = [
        send(gsend.at[d], pages.at[8 - d], pages.at[8 - d], ghosts[d]) for d in range(8)
    ]

    emb8[0:SPECIES, :] = emb[...]
    kinds8 = emb8[...]
    for r in range(BASIS):
        w2[8 * r : 8 * r + 8, :] = wrad[r : r + 1, :] * kinds8 * (1.0 / SLOTS)
    onehot = (spec[0] == iota((8, 128), 0)).astype(F32)
    start = dot(onehot, kinds8, 0, 0, HIGHEST)

    wait_mate.wait_recv()
    column = col.astype(F32) * CELL_EDGE
    offsets = (
        (row.astype(F32) * CELL_EDGE, column, 0.0),
        ((row + 1 - 2 * q).astype(F32) * CELL_EDGE, column, 0.0),
    )
    for side, ref in enumerate((own, mate)):
        for d in range(3):
            turn = (ref[d : d + 1, :] + offsets[side][d]) * (1.0 / LENGTHS[d])
            for p in range(3):
                piece = turn.astype(BF16).astype(F32)
                umat[3 * p + d : 3 * p + d + 1, 128 * side : 128 * side + 128] = piece
                turn = turn - piece
    fractions = umat[...].astype(BF16)

    def trig(i, carry):
        block = nmat[:, pl.ds(pl.multiple_of(q * 512 + i * 128, 128), 128)].astype(BF16)
        turns = dot(block, fractions, 0, 0)
        turns = turns - jnp.floor(turns + 0.5)
        w = turns * turns
        for f, value in enumerate((horner(COSINE, w), horner(SINE, w) * turns)):
            tab[f, i] = value.reshape(4, 32, 256)
            hi, lo = halves(value)
            thi[f, i] = hi.reshape(4, 32, 256)
            tlo[f, i] = lo.reshape(4, 32, 256)
            for side in range(2):
                mine = slice(128 * side, 128 * side + 128)
                for p, half in enumerate((hi, lo, hi)):
                    at = 384 * side + 128 * p
                    tsplit[f, i, :, at : at + 128] = half[:, mine]
        for d in range(3):
            nb[d, i] = dot(block, (iota((16, 128), 0) == d).astype(F32).astype(BF16), 0, 0).reshape(
                4, 32, 128
            )
        return carry

    lax.fori_loop(0, 4, trig, 0)

    for w in waits:
        w.wait_recv()
    live = cnt[0]
    rows8 = iota((8, 128), 0)

    def edge(g, carry):
        at = pl.multiple_of(g * 8, 8)
        index = nbr[0, 0, pl.ds(at, 8), :]
        page = lax.shift_right_logical(index, 7)
        lane = lax.bitwise_and(index, 127)
        picked = [jnp.zeros((8, 128), F32)] * 4
        for p in range(9):
            here = page == p
            for d in range(4):
                line = pages[p, d : d + 1, :]
                if p > 0 and d < 2 and DIRECTIONS[p - 1][d]:
                    line = line + CELL_EDGE * DIRECTIONS[p - 1][d]
                found = jnp.take_along_axis(
                    jnp.broadcast_to(line, (8, 128)), lane, axis=1, mode="promise_in_bounds"
                )
                picked[d] = jnp.where(here, found, picked[d])
        square = jnp.zeros((8, 128), F32)
        for d in range(3):
            v = picked[d] - pos[d, 0]
            vec[d, pl.ds(at, 8), :] = v
            square = square + v * v
        dist[pl.ds(at, 8), :] = square
        kinds[pl.ds(at, 8), :] = jnp.where(rows8 + at < live, picked[3], -1.0)
        return carry

    lax.fori_loop(0, 8, edge, 0, unroll=2)

    def radial(r, rate):
        e = jnp.exp(dist[...] * (-rate))
        expo[r] = e
        k = kinds[...]
        tile = jnp.zeros((8, 128), F32)
        for s in range(SPECIES):
            total = jnp.sum(jnp.where(k == s, e, 0.0), axis=0, keepdims=True)
            tile = jnp.where(rows8 == s, total, tile)
        basis[pl.ds(pl.multiple_of(r * 8, 8), 8), :] = tile
        return rate * GROWTH

    lax.fori_loop(0, BASIS, radial, jnp.float32(RATE), unroll=4)

    aggregate = dot(basis[...], w2[...], 0, 0, HIGH)
    u = dot(aggregate, wmix[...], 1, 0, HIGH)
    gate = 1.0 / (1.0 + jnp.exp(-u))
    mine = start + u * gate
    upd[0:128, :] = mine
    wait_mate = send(upd.at[0:128], upd.at[128:256], upd.at[128:256], partner)
    dsilu[...] = (gate * (1.0 + u * (1.0 - gate))).T
    p = dot(mine, wread[...], 1, 0, HIGH)
    gate = 1.0 / (1.0 + jnp.exp(-p))
    gshort[...] = dot(wread[...], wout[...] * (gate * (1.0 + p * (1.0 - gate))), 1, 1, HIGH)

    def split(side):
        value = upd[128 * side : 128 * side + 128, :]
        hi, lo = halves(value)
        for p, half in enumerate((hi, hi, lo)):
            usplit[384 * side + 128 * p : 384 * side + 128 * p + 128, :] = half

    def split_turned(side):
        hi, lo = halves(upd[128 * side : 128 * side + 128, :].T)
        for p, half in enumerate((hi, hi, lo)):
            uturn[128 * p : 128 * p + 128, 128 * side : 128 * side + 128] = half

    split(0)
    wait_mate.wait_recv()
    split(1)

    places = (xs, ys)
    seconds = (ys, xs)
    along = (along_x, along_y)
    order = (2, 1, 3, 0)
    waits1 = {}
    for off in order:
        chunks = [places[f][off] for f in range(2)]
        lines = jnp.concatenate([tsplit[f, chunks[f]] for f in range(2)], axis=0)
        value = dot(lines, usplit[...], 1, 0).reshape(2, 4, 32, 128)
        for f in range(2):
            chunk = chunks[f]
            sums[f, chunk] = value[f]
            if off == 0:
                continue
            for off2 in order:
                waits1[f, off, off2] = send(
                    sums.at[f, chunk, seconds[f][off2]],
                    in1.at[f, off - 1, off2],
                    in1.at[f, off - 1, off2],
                    along[f](off),
                )
    waits2 = {}
    for off2 in order:
        for f in range(2):
            for off in (1, 3, 2):
                waits1[f, off, off2].wait_recv()
            total = (
                sums[f, places[f][0], seconds[f][off2]]
                + in1[f, 0, off2]
                + in1[f, 1, off2]
                + in1[f, 2, off2]
            )
            if off2 == 0:
                zbuf[32 * f : 32 * f + 32, :] = total
                continue
            part[f, off2] = total
            waits2[f, off2] = send(
                part.at[f, off2], in2.at[f, off2 - 1], in2.at[f, off2 - 1], along[1 - f](off2)
            )
    for f in range(2):
        for off2 in (1, 3, 2):
            waits2[f, off2].wait_recv()
        zbuf[32 * f : 32 * f + 32, :] += in2[f, 0] + in2[f, 1] + in2[f, 2]
    waits = []
    for off in (4, 3, 5, 2, 6, 1, 7):
        at = pl.ds(pl.multiple_of(zs[off] * 8, 8), 8)
        waits.append(send(zbuf.at[at], zin.at[off - 1], zin.at[off - 1], along_z(off)))

    first = 512 * q + (1 - zh) * (128 * x + 32 * y) + zh * (128 * y + 32 * x) + 8 * zl
    chosen = (iota((8, 1024), 1) == iota((8, 1024), 0) + first).astype(BF16)
    mine = dot(chosen, nmat[...].astype(BF16), 1, 1)
    k_of = [mine[:, d : d + 1] * (2.0 * math.pi / LENGTHS[d]) for d in range(3)]
    norm = k_of[0] * k_of[0] + k_of[1] * k_of[1] + k_of[2] * k_of[2]
    inside = lax.div(first, WAVES)
    source = pl.multiple_of(first - inside * WAVES, 8)
    weight = amp[...] * gain[pl.ds(source, 8), :] * jnp.exp(-width[...] * norm)
    weight = jnp.where(rows8 + first < WAVES, weight * (1.0 / VOLUME), 0.0)

    rows128 = iota((128, 128), 0)

    def mark(g, carry):
        for s in range(4):
            lane = lax.bitwise_and(nbr[0, 0, pl.ds(g * 4 + s, 1), :], 127)
            marks[g, :, 128 * s : 128 * s + 128] = (rows128 == lane).astype(F32).astype(BF16)
        return carry

    lax.fori_loop(0, 16, mark, 0)
    for d in range(8):
        gmarks[:, 128 * d : 128 * d + 128] = (
            (rows128 == gidx[0, 0, d : d + 1, :]).astype(F32).astype(BF16)
        )

    split_turned(0)
    split_turned(1)
    for m, (a, b) in enumerate(PAIRS):
        pair[m] = vec[a] * vec[b]

    def moments(r, rate):
        e = expo[r] * (2.0 * rate)
        k = kinds[...]
        parts = [jnp.where(k == s, e, 0.0) for s in range(SPECIES)]
        for m in range(6):
            v = pair[m]
            tile = jnp.zeros((8, 128), F32)
            for s in range(SPECIES):
                total = jnp.sum(parts[s] * v, axis=0, keepdims=True)
                tile = jnp.where(rows8 == s, total, tile)
            moment[m, pl.ds(pl.multiple_of(r * 8, 8), 8), :] = tile
        return rate * GROWTH

    lax.fori_loop(0, BASIS, moments, jnp.float32(RATE))

    for w in waits:
        w.wait_recv()
    total = zbuf[pl.ds(pl.multiple_of(z * 8, 8), 8), :]
    for i in range(7):
        total = total + zin[i]
    result = weight * total
    mine_z = pl.ds(pl.multiple_of(z * 8, 8), 8)
    c3[mine_z, :] = result
    waits = []
    for off in (4, 3, 5, 2, 6, 1, 7):
        at = pl.ds(pl.multiple_of(zs[8 - off] * 8, 8), 8)
        waits.append(send(c3.at[mine_z], c3.at[mine_z], c3.at[at], along_z(off)))

    power = result * total
    strain = jnp.sum(width[...] * power, axis=1, keepdims=True)
    energy = 0.5 * jnp.sum(jnp.sum(power, axis=1, keepdims=True), axis=0, keepdims=True)
    lanes = iota((1, 128), 1)
    tile = jnp.where((lanes == 0) | (lanes == 4) | (lanes == 8), energy, 0.0)
    for a, b in PAIRS:
        s = jnp.sum(k_of[a] * k_of[b] * strain, axis=0, keepdims=True)
        tile = tile - jnp.where((lanes == 3 * a + b) | (lanes == 3 * b + a), s, 0.0)

    turned_mix = wmix[...].T
    for m in range(6):
        answer = dot(w2[...], moment[m], 0, 0, HIGH)
        uvir[0, m] = dot(turned_mix, answer, 1, 0, HIGH) * dsilu[...]
    wait_uvir = send(uvir.at[0], uvir.at[1], uvir.at[1], partner)
    fgrad[...] = jnp.zeros((128, 256), F32)
    cgrad[...] = jnp.zeros((3, 8, 256), F32)

    for w in waits:
        w.wait_recv()

    rounds = (1, 3, 2)
    waits2, waits1 = {}, {}

    def spread(f, off2, piece, src):
        for off in (2, 1, 3):
            waits1[f, off, off2] = send(
                src,
                coef.at[f, places[f][0], piece],
                coef.at[f, places[f][4 - off], piece],
                along[f](off),
            )

    for off2 in (2, 1, 3):
        for f in range(2):
            waits2[f, off2] = send(
                c3.at[32 * f : 32 * f + 32],
                coef.at[f, places[f][0], seconds[f][0]],
                coef.at[f, places[f][0], seconds[f][(4 - off2) % 4]],
                along[1 - f](off2),
            )
    for f in range(2):
        spread(f, 0, seconds[f][0], c3.at[32 * f : 32 * f + 32])
        coef[f, places[f][0], seconds[f][0]] = c3[32 * f : 32 * f + 32, :]
    for off2 in rounds:
        for f in range(2):
            waits2[f, off2].wait_recv()
            piece = seconds[f][(4 - off2) % 4]
            spread(f, off2, piece, coef.at[f, places[f][0], piece])

    def back(f, piece):
        c = coef[f, :, piece].reshape(128, 128)
        hi, lo = halves(c.T)
        t = thi[f, :, piece].reshape(128, 256)
        fgrad[...] += dot(
            jnp.concatenate([hi, hi, lo], axis=1),
            jnp.concatenate([t, tlo[f, :, piece].reshape(128, 256), t], axis=0),
            1,
            0,
        )
        hi, lo = halves(c)
        turned = dot(jnp.concatenate([hi, lo, hi], axis=1), uturn[...], 1, 0)
        turned = turned * tab[1 - f, :, piece].reshape(128, 256)
        if f == 0:
            turned = -turned
        for d in range(3):
            n = nb[d, :, piece].reshape(128, 128)
            for side in range(2):
                mine = slice(128 * side, 128 * side + 128)
                cgrad[d, :, mine] += jnp.sum((turned[:, mine] * n).reshape(16, 8, 128), axis=0)

    for off2 in (0,) + rounds:
        for f in range(2):
            for off in rounds:
                waits1[f, off, off2].wait_recv()
            back(f, seconds[f][(4 - off2) % 4])
    xout[0:128, :] = fgrad[:, 128:256]
    for d in range(3):
        xout[128 + 8 * d : 136 + 8 * d, :] = cgrad[d, :, 128:256]
    wait_mate = send(xout, xin, xin, partner)

    def gather(buffer, value, me, to, come, offs):
        buffer[me] = value
        return [
            send(buffer.at[me], buffer.at[me], buffer.at[come(off)], to(off)) for off in offs
        ]

    def add_up(buffer):
        value = buffer[0]
        for i in range(1, 16):
            value = value + buffer[i]
        return value

    fown = fgrad[:, 0:128] + gshort[...]
    wait_uvir.wait_recv()
    for m, (a, b) in enumerate(PAIRS):
        s = jnp.sum(fown * uvir[0, m] + fgrad[:, 128:256] * uvir[1, m], axis=0, keepdims=True)
        s = jnp.sum(s, axis=1, keepdims=True)
        tile = tile + jnp.where((lanes == 3 * a + b) | (lanes == 3 * b + a), s, 0.0)
    waits_v = gather(va, tile, m_zq, among_zq, from_zq, FAR_ZQ)
    wait_mate.wait_recv()

    du = (fown + xin[0:128, :]) * dsilu[...]
    daggregate = dot(wmix[...], du, 1, 0, HIGH)
    basis[...] = dot(w2[...], daggregate, 1, 0, HIGH)

    def radial_back(r, carry):
        rate, grad = carry
        d = basis[pl.ds(pl.multiple_of(r * 8, 8), 8), :] * (-2.0 * rate)
        k = kinds[...]
        chosen = jnp.zeros((SLOTS, 128), F32)
        for s in range(SPECIES):
            chosen = jnp.where(k == s, d[s : s + 1, :], chosen)
        return rate * GROWTH, grad + chosen * expo[r]

    _, slope = lax.fori_loop(
        0, BASIS, radial_back, (jnp.float32(RATE), jnp.zeros((SLOTS, 128), F32)), unroll=4
    )
    spent = []
    for d in range(3):
        g = slope * vec[d]
        vgrad[d] = g
        spent.append(jnp.sum(g, axis=0, keepdims=True))

    rows16 = iota((16, 128), 0)

    def scatter(g, total):
        left = []
        for s in range(4):
            at = pl.ds(g * 4 + s, 1)
            page = lax.shift_right_logical(nbr[0, 0, at, :], 7)
            lines = jnp.concatenate(
                [jnp.where(rows16 == page, vgrad[d, at, :], 0.0) for d in range(3)], axis=0
            )
            left.append(jnp.concatenate(halves(lines), axis=0))
        return total + dot(jnp.concatenate(left, axis=1), marks[g], 1, 1)

    total = lax.fori_loop(0, SLOTS // 4, scatter, jnp.zeros((96, 128), F32), unroll=2)
    tgrad[...] = total[0:48, :] + total[48:96, :]
    for p in range(8):
        for d in range(3):
            gback[p, d : d + 1, :] = tgrad[16 * d + p + 1 : 16 * d + p + 2, :]
    waits_g = [send(gback.at[p], gret.at[7 - p], gret.at[7 - p], ghosts[p]) for p in range(8)]

    for w in waits_v:
        w.wait_recv()
    waits_v = gather(vb, add_up(va), m_xy, among_xy, from_xy, FAR_XY)
    for w in waits_g:
        w.wait_recv()
    left = []
    for d in range(8):
        hi, lo = halves(jnp.concatenate([gret[d], jnp.zeros((8, 128), F32)], axis=0))
        left.append(jnp.concatenate([hi, lo], axis=0))
    back_home = dot(jnp.concatenate(left, axis=1), gmarks[...], 1, 1)
    back_home = back_home[0:16, :] + back_home[16:32, :]
    moved = [
        jnp.sum(
            cgrad[d, :, 0:128] + xin[128 + 8 * d : 136 + 8 * d, :], axis=0, keepdims=True
        )
        for d in range(3)
    ]
    for d in range(3):
        grad = (
            tgrad[16 * d : 16 * d + 1, :]
            - spent[d]
            + moved[d] * (2.0 * math.pi / LENGTHS[d])
            + back_home[d : d + 1, :]
        )
        out[d : d + 1, :] = -grad
    for w in waits_v:
        w.wait_recv()
    out[4:5, :] = add_up(vb) * (1.0 / VOLUME)
    for copy in started:
        copy.wait_send()


def hand_over(result, force, virial):
    for d in range(3):
        force[d, 0] = result[d : d + 1, :]
    for d in range(3):
        virial[d : d + 1, :] = result[4:5, 3 * d : 3 * d + 3]


def per_device(
    positions, species, counts, neighbours, ghost_index, wave_numbers, embedding,
    w_radial, w_mix, w_read, w_out, amplitude, kernel_width, filter_gain,
):
    result = pl.pallas_call(
        kernel,
        out_shape=pltpu.VMEM((8, 128), F32),
        in_specs=[pl.BlockSpec(memory_space=pltpu.HBM)] * 14,
        out_specs=pl.BlockSpec(memory_space=pltpu.VMEM),
        scratch_shapes=[pltpu.VMEM(shape, dtype) for shape, dtype in INPUTS]
        + [pltpu.VMEM(shape, dtype) for _, shape, dtype in SCRATCH]
        + [
            pltpu.SemaphoreType.DMA((N_COPIES,)),
            pltpu.SemaphoreType.DMA((N_COPIES,)),
            pltpu.SemaphoreType.DMA((14,)),
        ],
        compiler_params=pltpu.CompilerParams(collective_id=0, has_side_effects=True),
        name="ewald",
    )(
        positions, species, counts, neighbours, ghost_index, wave_numbers, embedding,
        w_radial, w_mix, w_read, w_out.reshape(1, 128), amplitude.reshape(1, 128),
        kernel_width.reshape(1, 128), filter_gain,
    )
    return pl.pallas_call(
        hand_over,
        out_shape=(
            jax.ShapeDtypeStruct((3, 1, 1, 128), F32),
            jax.ShapeDtypeStruct((3, 3), F32),
        ),
        in_specs=[pl.BlockSpec(memory_space=pltpu.VMEM)],
        out_specs=(
            pl.BlockSpec(memory_space=pltpu.VMEM),
            pl.BlockSpec(memory_space=pltpu.VMEM),
        ),
        name="hand_over",
    )(pltpu.with_memory_space_constraint(result, pltpu.VMEM))


def solution(mesh):
    return jax.shard_map(
        per_device,
        mesh=mesh,
        in_specs=(
            P(None, "row", "col", None),
            P("row", "col", None),
            P("row", "col", None),
            P("row", "col", None, None),
            P("row", "col", None, None),
            P(), P(), P(), P(), P(), P(), P(), P(), P(),
        ),
        out_specs=(P(None, "row", "col", None), P()),
        check_vma=False,
    )
```

```python
import functools
import math

import jax
import jax.numpy as jnp
from jax import lax
from jax.experimental import pallas as pl
from jax.experimental.pallas import tpu as pltpu
from jax.sharding import PartitionSpec as P

CELL_EDGE = 12.0
HEIGHT = 36.0
ROWS = 32
COLS = 8
VOLUME = CELL_EDGE * ROWS * CELL_EDGE * COLS * HEIGHT
LENGTHS = (CELL_EDGE * ROWS, CELL_EDGE * COLS, HEIGHT)
DIRECTIONS = ((-1, -1), (-1, 0), (-1, 1), (0, -1), (0, 1), (1, -1), (1, 0), (1, 1))
RATE = 0.003
GROWTH = 1.6
BASIS = 16
SPECIES = 6
SLOTS = 64
WAVES = 1000
HIGH = lax.Precision.HIGH
HIGHEST = lax.Precision.HIGHEST
MESH = pl.DeviceIdType.MESH
F32 = jnp.float32
BF16 = jnp.bfloat16
SINE = (
    6.2831854820251465,
    -41.34170150756836,
    81.60513305664062,
    -76.70301818847656,
    42.02592849731445,
    -14.899847030639648,
    3.2381374835968018,
)
COSINE = (
    1.0,
    -19.73920440673828,
    64.93911743164062,
    -85.45014190673828,
    60.16762924194336,
    -25.967599868774414,
    6.528658390045166,
)
def dot(a, b, ca, cb, precision=None):
    return lax.dot_general(
        a, b, (((ca,), (cb,)), ((), ())), precision=precision, preferred_element_type=F32
    )


def horner(coefs, w):
    value = jnp.full_like(w, coefs[-1])
    for c in coefs[-2::-1]:
        value = value * w + c
    return value


def halves(x):
    hi = x.astype(BF16)
    lo = (x - hi.astype(F32)).astype(BF16)
    return hi, lo


def iota(shape, dim):
    return lax.broadcasted_iota(jnp.int32, shape, dim)


N_COPIES = 132
FAR_ZQ = (9, 8, 7, 6, 11, 10, 5, 4, 13, 12, 3, 2, 15, 14, 1)
FAR_XY = (10, 9, 11, 6, 14, 5, 7, 13, 15, 8, 2, 4, 12, 1, 3)
PAIRS = ((0, 0), (0, 1), (0, 2), (1, 1), (1, 2), (2, 2))
INPUTS = (
    ((3, 1, 1, 128), F32), ((1, 1, 128), jnp.int32), ((1, 1, 128), jnp.int32),
    ((1, 1, 64, 128), jnp.int32), ((1, 1, 8, 128), jnp.int32), ((3, 1000), jnp.int32),
    ((6, 128), F32), ((16, 128), F32), ((128, 128), F32), ((128, 128), F32), ((1, 128), F32),
    ((1, 128), F32), ((1, 128), F32), ((1000, 128), F32),
)
SCRATCH = (
    ("own", (8, 128), F32), ("mate", (8, 128), F32), ("gsend", (8, 8, 128), F32),
    ("pages", (9, 8, 128), F32), ("gback", (8, 8, 128), F32), ("gret", (8, 8, 128), F32),
    ("nmat", (16, 1024), F32), ("umat", (16, 256), F32), ("tab", (2, 4, 4, 32, 256), F32),
    ("tsplit", (2, 4, 128, 768), BF16), ("thi", (2, 4, 4, 32, 256), BF16),
    ("tlo", (2, 4, 4, 32, 256), BF16), ("nb", (3, 4, 4, 32, 128), F32),
    ("emb8", (8, 128), F32), ("w2", (128, 128), F32),
    ("vec", (3, 64, 128), F32), ("kinds", (64, 128), F32), ("dist", (64, 128), F32),
    ("expo", (16, 64, 128), F32), ("basis", (128, 128), F32), ("upd", (256, 128), F32),
    ("usplit", (768, 128), BF16), ("uturn", (384, 256), BF16),
    ("dsilu", (128, 128), F32), ("gshort", (128, 128), F32),
    ("sums", (2, 4, 4, 32, 128), F32), ("in1", (2, 3, 4, 32, 128), F32),
    ("part", (2, 4, 32, 128), F32), ("in2", (2, 3, 32, 128), F32),
    ("zin", (7, 8, 128), F32), ("zbuf", (64, 128), F32), ("c3", (64, 128), F32),
    ("coef", (2, 4, 4, 32, 128), F32), ("fgrad", (128, 256), F32), ("cgrad", (3, 8, 256), F32),
    ("xout", (152, 128), F32), ("xin", (152, 128), F32),
    ("marks", (16, 128, 512), BF16), ("gmarks", (128, 1024), BF16),
    ("vgrad", (3, 64, 128), F32), ("tgrad", (48, 128), F32),
    ("pair", (6, 64, 128), F32), ("moment", (6, 128, 128), F32),
    ("uvir", (2, 6, 128, 128), F32),
    ("va", (16, 1, 128), F32), ("vb", (16, 1, 128), F32),
)


def kernel(*refs):
    ins, out = refs[:14], refs[14]
    here = refs[15:29]
    named = refs[29 : 29 + len(SCRATCH)]
    ssem, rsem, lsem = refs[29 + len(SCRATCH) :]
    (pos, spec, cnt, nbr, gidx, wn, emb, wrad, wmix, wread, wout, amp, width, gain) = here
    (
        own, mate, gsend, pages, gback, gret, nmat, umat, tab, tsplit, thi, tlo, nb, emb8, w2,
        vec, kinds, dist, expo, basis, upd, usplit, uturn, dsilu, gshort,
        sums, in1, part, in2, zin, zbuf, c3, coef, fgrad, cgrad, xout, xin,
        marks, gmarks, vgrad, tgrad, pair, moment, uvir, va, vb,
    ) = named
    row = lax.axis_index("row")
    col = lax.axis_index("col")
    q = lax.rem(row, 2)
    zl = lax.rem(lax.div(row, 2), 4)
    y = lax.div(row, 8)
    x = lax.rem(col, 4)
    zh = lax.div(col, 4)
    z = zh * 4 + zl

    xs = [x] + [lax.rem(x + off, 4) for off in (1, 2, 3)]
    ys = [y] + [lax.rem(y + off, 4) for off in (1, 2, 3)]
    zs = [z] + [lax.rem(z + off, 8) for off in range(1, 8)]
    z_cols = [lax.div(at, 4) * 4 for at in zs]
    z_rows = [(at - high) * 2 for at, high in zip(zs, z_cols)]
    y_rows = [at * 8 for at in ys]
    cores = [q, 1 - q]
    x_base = z_cols[0]
    y_base = z_rows[0] + q

    up, down = lax.rem(row + 1, ROWS), lax.rem(row + ROWS - 1, ROWS)
    east, west = lax.rem(col + 1, COLS), lax.rem(col + COLS - 1, COLS)
    ghosts = [((down, row, up)[a + 1], (west, col, east)[b + 1]) for a, b in DIRECTIONS]
    partner = (row + 1 - 2 * q, col)

    def along_x(off):
        return (row, x_base + xs[off])

    def along_y(off):
        return (y_rows[off] + y_base, col)

    def along_z(off):
        return (y_rows[0] + z_rows[off] + q, z_cols[off] + x)

    def among_zq(off):
        dz, dq = off // 2, off % 2
        return (y_rows[0] + z_rows[dz] + cores[dq], z_cols[dz] + x)

    def among_xy(off):
        dx, dy = off // 4, off % 4
        return (y_rows[dy] + y_base, x_base + xs[dx])

    m_zq = z * 2 + q
    m_xy = x * 4 + y

    def from_zq(off):
        dz, dq = off // 2, off % 2
        return zs[(8 - dz) % 8] * 2 + cores[dq]

    def from_xy(off):
        dx, dy = off // 4, off % 4
        return xs[(4 - dx) % 4] * 4 + ys[(4 - dy) % 4]

    loads = [pltpu.make_async_copy(ins[i], here[i], lsem.at[i]) for i in range(14)]
    for i in (0, 1, 4, 2, 3, 5, 6, 7, 8, 9, 10, 11, 12, 13):
        loads[i].start()
    barrier = pltpu.get_barrier_semaphore()
    greeted = (
        ghosts + [among_zq(off) for off in FAR_ZQ] + [among_xy(off) for off in FAR_XY]
    )
    for who in greeted:
        pl.semaphore_signal(barrier, inc=1, device_id=who, device_id_type=MESH)

    started = []

    def send(src, dst, landing, who):
        i = len(started)
        copy = pltpu.make_async_remote_copy(
            src_ref=src,
            dst_ref=dst,
            send_sem=ssem.at[i],
            recv_sem=rsem.at[i],
            device_id=who,
            device_id_type=MESH,
        )
        copy.start()
        started.append(copy)
        return pltpu.make_async_remote_copy(
            src_ref=src,
            dst_ref=landing,
            send_sem=ssem.at[i],
            recv_sem=rsem.at[i],
            device_id=who,
            device_id_type=MESH,
        )

    gback[...] = jnp.zeros((8, 8, 128), F32)
    nmat[...] = jnp.zeros((16, 1024), F32)
    umat[...] = jnp.zeros((16, 256), F32)
    emb8[...] = jnp.zeros((8, 128), F32)
    own[...] = jnp.zeros((8, 128), F32)
    for i in (0, 1, 4):
        loads[i].wait()

    for d in range(3):
        own[d : d + 1, :] = pos[d, 0]
    own[3:4, :] = spec[0].astype(F32)
    table = own[...]
    for d in range(8):
        index = jnp.broadcast_to(gidx[0, 0, d : d + 1, :], (8, 128))
        gsend[d] = jnp.take_along_axis(table, index, axis=1, mode="promise_in_bounds")
    pages[0] = table
    pl.semaphore_wait(barrier, len(greeted))
    wait_mate = send(own, mate, mate, partner)
    waits = [
        send(gsend.at[d], pages.at[8 - d], pages.at[8 - d], ghosts[d]) for d in range(8)
    ]

    for i in (2, 3, 5, 6, 7, 8, 9, 10, 11, 12, 13):
        loads[i].wait()
    numbers = wn[...].astype(F32)
    for p in range(3):
        nmat[3 * p : 3 * p + 3, 0:WAVES] = numbers

    emb8[0:SPECIES, :] = emb[...]
    kinds8 = emb8[...]
    for r in range(BASIS):
        w2[8 * r : 8 * r + 8, :] = wrad[r : r + 1, :] * kinds8 * (1.0 / SLOTS)
    onehot = (spec[0] == iota((8, 128), 0)).astype(F32)
    start = dot(onehot, kinds8, 0, 0, HIGHEST)

    wait_mate.wait_recv()
    column = col.astype(F32) * CELL_EDGE
    offsets = (
        (row.astype(F32) * CELL_EDGE, column, 0.0),
        ((row + 1 - 2 * q).astype(F32) * CELL_EDGE, column, 0.0),
    )
    for side, ref in enumerate((own, mate)):
        for d in range(3):
            turn = (ref[d : d + 1, :] + offsets[side][d]) * (1.0 / LENGTHS[d])
            for p in range(3):
                piece = turn.astype(BF16).astype(F32)
                umat[3 * p + d : 3 * p + d + 1, 128 * side : 128 * side + 128] = piece
                turn = turn - piece
    fractions = umat[...].astype(BF16)

    def trig(i, carry):
        block = nmat[:, pl.ds(pl.multiple_of(q * 512 + i * 128, 128), 128)].astype(BF16)
        turns = dot(block, fractions, 0, 0)
        turns = turns - jnp.floor(turns + 0.5)
        w = turns * turns
        for f, value in enumerate((horner(COSINE, w), horner(SINE, w) * turns)):
            tab[f, i] = value.reshape(4, 32, 256)
            hi, lo = halves(value)
            thi[f, i] = hi.reshape(4, 32, 256)
            tlo[f, i] = lo.reshape(4, 32, 256)
            for side in range(2):
                mine = slice(128 * side, 128 * side + 128)
                for p, half in enumerate((hi, lo, hi)):
                    at = 384 * side + 128 * p
                    tsplit[f, i, :, at : at + 128] = half[:, mine]
        for d in range(3):
            nb[d, i] = dot(block, (iota((16, 128), 0) == d).astype(F32).astype(BF16), 0, 0).reshape(
                4, 32, 128
            )
        return carry

    lax.fori_loop(0, 4, trig, 0)

    for w in waits:
        w.wait_recv()
    live = cnt[0]
    rows8 = iota((8, 128), 0)

    def edge(g, carry):
        at = pl.multiple_of(g * 8, 8)
        index = nbr[0, 0, pl.ds(at, 8), :]
        page = lax.shift_right_logical(index, 7)
        lane = lax.bitwise_and(index, 127)
        picked = [jnp.zeros((8, 128), F32)] * 4
        for p in range(9):
            here = page == p
            for d in range(4):
                line = pages[p, d : d + 1, :]
                if p > 0 and d < 2 and DIRECTIONS[p - 1][d]:
                    line = line + CELL_EDGE * DIRECTIONS[p - 1][d]
                found = jnp.take_along_axis(
                    jnp.broadcast_to(line, (8, 128)), lane, axis=1, mode="promise_in_bounds"
                )
                picked[d] = jnp.where(here, found, picked[d])
        square = jnp.zeros((8, 128), F32)
        for d in range(3):
            v = picked[d] - pos[d, 0]
            vec[d, pl.ds(at, 8), :] = v
            square = square + v * v
        dist[pl.ds(at, 8), :] = square
        kinds[pl.ds(at, 8), :] = jnp.where(rows8 + at < live, picked[3], -1.0)
        return carry

    lax.fori_loop(0, 8, edge, 0, unroll=2)

    def radial(r, rate):
        e = jnp.exp(dist[...] * (-rate))
        expo[r] = e
        k = kinds[...]
        tile = jnp.zeros((8, 128), F32)
        for s in range(SPECIES):
            total = jnp.sum(jnp.where(k == s, e, 0.0), axis=0, keepdims=True)
            tile = jnp.where(rows8 == s, total, tile)
        basis[pl.ds(pl.multiple_of(r * 8, 8), 8), :] = tile
        return rate * GROWTH

    lax.fori_loop(0, BASIS, radial, jnp.float32(RATE), unroll=4)

    aggregate = dot(basis[...], w2[...], 0, 0, HIGH)
    u = dot(aggregate, wmix[...], 1, 0, HIGH)
    gate = 1.0 / (1.0 + jnp.exp(-u))
    mine = start + u * gate
    upd[0:128, :] = mine
    wait_mate = send(upd.at[0:128], upd.at[128:256], upd.at[128:256], partner)
    dsilu[...] = (gate * (1.0 + u * (1.0 - gate))).T
    p = dot(mine, wread[...], 1, 0, HIGH)
    gate = 1.0 / (1.0 + jnp.exp(-p))
    gshort[...] = dot(wread[...], wout[...] * (gate * (1.0 + p * (1.0 - gate))), 1, 1, HIGH)

    def split(side):
        value = upd[128 * side : 128 * side + 128, :]
        hi, lo = halves(value)
        for p, half in enumerate((hi, hi, lo)):
            usplit[384 * side + 128 * p : 384 * side + 128 * p + 128, :] = half

    def split_turned(side):
        hi, lo = halves(upd[128 * side : 128 * side + 128, :].T)
        for p, half in enumerate((hi, hi, lo)):
            uturn[128 * p : 128 * p + 128, 128 * side : 128 * side + 128] = half

    split(0)
    for i in range(4):
        lines = jnp.concatenate([tsplit[f, i, :, 0:384] for f in range(2)], axis=0)
        value = dot(lines, usplit[0:384, :], 1, 0).reshape(2, 4, 32, 128)
        for f in range(2):
            sums[f, i] = value[f]
    wait_mate.wait_recv()
    split(1)

    places = (xs, ys)
    seconds = (ys, xs)
    along = (along_x, along_y)
    order = (2, 1, 3, 0)
    waits1 = {}
    for off in order:
        chunks = [places[f][off] for f in range(2)]
        lines = jnp.concatenate([tsplit[f, chunks[f], :, 384:768] for f in range(2)], axis=0)
        value = dot(lines, usplit[384:768, :], 1, 0).reshape(2, 4, 32, 128)
        for f in range(2):
            chunk = chunks[f]
            sums[f, chunk] += value[f]
            if off == 0:
                continue
            for off2 in order:
                waits1[f, off, off2] = send(
                    sums.at[f, chunk, seconds[f][off2]],
                    in1.at[f, off - 1, off2],
                    in1.at[f, off - 1, off2],
                    along[f](off),
                )
    waits2 = {}
    for off2 in order:
        for f in range(2):
            for off in (1, 3, 2):
                waits1[f, off, off2].wait_recv()
            total = (
                sums[f, places[f][0], seconds[f][off2]]
                + in1[f, 0, off2]
                + in1[f, 1, off2]
                + in1[f, 2, off2]
            )
            if off2 == 0:
                zbuf[32 * f : 32 * f + 32, :] = total
                continue
            part[f, off2] = total
            waits2[f, off2] = send(
                part.at[f, off2], in2.at[f, off2 - 1], in2.at[f, off2 - 1], along[1 - f](off2)
            )
    for f in range(2):
        for off2 in (1, 3, 2):
            waits2[f, off2].wait_recv()
        zbuf[32 * f : 32 * f + 32, :] += in2[f, 0] + in2[f, 1] + in2[f, 2]
    waits = []
    for off in (4, 3, 5, 2, 6, 1, 7):
        at = pl.ds(pl.multiple_of(zs[off] * 8, 8), 8)
        waits.append(send(zbuf.at[at], zin.at[off - 1], zin.at[off - 1], along_z(off)))

    first = 512 * q + (1 - zh) * (128 * x + 32 * y) + zh * (128 * y + 32 * x) + 8 * zl
    chosen = (iota((8, 1024), 1) == iota((8, 1024), 0) + first).astype(BF16)
    mine = dot(chosen, nmat[...].astype(BF16), 1, 1)
    k_of = [mine[:, d : d + 1] * (2.0 * math.pi / LENGTHS[d]) for d in range(3)]
    norm = k_of[0] * k_of[0] + k_of[1] * k_of[1] + k_of[2] * k_of[2]
    inside = lax.div(first, WAVES)
    source = pl.multiple_of(first - inside * WAVES, 8)
    weight = amp[...] * gain[pl.ds(source, 8), :] * jnp.exp(-width[...] * norm)
    weight = jnp.where(rows8 + first < WAVES, weight * (1.0 / VOLUME), 0.0)

    rows128 = iota((128, 128), 0)

    def mark(g, carry):
        for s in range(4):
            lane = lax.bitwise_and(nbr[0, 0, pl.ds(g * 4 + s, 1), :], 127)
            marks[g, :, 128 * s : 128 * s + 128] = (rows128 == lane).astype(F32).astype(BF16)
        return carry

    lax.fori_loop(0, 16, mark, 0)
    for d in range(8):
        gmarks[:, 128 * d : 128 * d + 128] = (
            (rows128 == gidx[0, 0, d : d + 1, :]).astype(F32).astype(BF16)
        )

    split_turned(0)
    split_turned(1)
    for m, (a, b) in enumerate(PAIRS):
        pair[m] = vec[a] * vec[b]

    def moments(r, rate):
        e = expo[r] * (2.0 * rate)
        k = kinds[...]
        parts = [jnp.where(k == s, e, 0.0) for s in range(SPECIES)]
        for m in range(6):
            v = pair[m]
            tile = jnp.zeros((8, 128), F32)
            for s in range(SPECIES):
                total = jnp.sum(parts[s] * v, axis=0, keepdims=True)
                tile = jnp.where(rows8 == s, total, tile)
            moment[m, pl.ds(pl.multiple_of(r * 8, 8), 8), :] = tile
        return rate * GROWTH

    lax.fori_loop(0, BASIS, moments, jnp.float32(RATE))

    for w in waits:
        w.wait_recv()
    total = zbuf[pl.ds(pl.multiple_of(z * 8, 8), 8), :]
    for i in range(7):
        total = total + zin[i]
    result = weight * total
    mine_z = pl.ds(pl.multiple_of(z * 8, 8), 8)
    c3[mine_z, :] = result
    waits = []
    for off in (4, 3, 5, 2, 6, 1, 7):
        at = pl.ds(pl.multiple_of(zs[8 - off] * 8, 8), 8)
        waits.append(send(c3.at[mine_z], c3.at[mine_z], c3.at[at], along_z(off)))

    power = result * total
    strain = jnp.sum(width[...] * power, axis=1, keepdims=True)
    energy = 0.5 * jnp.sum(jnp.sum(power, axis=1, keepdims=True), axis=0, keepdims=True)
    lanes = iota((1, 128), 1)
    tile = jnp.where((lanes == 0) | (lanes == 4) | (lanes == 8), energy, 0.0)
    for a, b in PAIRS:
        s = jnp.sum(k_of[a] * k_of[b] * strain, axis=0, keepdims=True)
        tile = tile - jnp.where((lanes == 3 * a + b) | (lanes == 3 * b + a), s, 0.0)

    turned_mix = wmix[...].T
    for m in range(6):
        answer = dot(w2[...], moment[m], 0, 0, HIGH)
        uvir[0, m] = dot(turned_mix, answer, 1, 0, HIGH) * dsilu[...]
    wait_uvir = send(uvir.at[0], uvir.at[1], uvir.at[1], partner)
    fgrad[...] = jnp.zeros((128, 256), F32)
    cgrad[...] = jnp.zeros((3, 8, 256), F32)

    for w in waits:
        w.wait_recv()

    rounds = (1, 3, 2)
    waits2, waits1 = {}, {}

    def spread(f, off2, piece, src):
        for off in (2, 1, 3):
            waits1[f, off, off2] = send(
                src,
                coef.at[f, places[f][0], piece],
                coef.at[f, places[f][4 - off], piece],
                along[f](off),
            )

    for off2 in (2, 1, 3):
        for f in range(2):
            waits2[f, off2] = send(
                c3.at[32 * f : 32 * f + 32],
                coef.at[f, places[f][0], seconds[f][0]],
                coef.at[f, places[f][0], seconds[f][(4 - off2) % 4]],
                along[1 - f](off2),
            )
    for f in range(2):
        spread(f, 0, seconds[f][0], c3.at[32 * f : 32 * f + 32])
        coef[f, places[f][0], seconds[f][0]] = c3[32 * f : 32 * f + 32, :]
    for off2 in rounds:
        for f in range(2):
            waits2[f, off2].wait_recv()
            piece = seconds[f][(4 - off2) % 4]
            spread(f, off2, piece, coef.at[f, places[f][0], piece])

    def back(f, piece):
        c = coef[f, :, piece].reshape(128, 128)
        hi, lo = halves(c.T)
        t = thi[f, :, piece].reshape(128, 256)
        fgrad[...] += dot(
            jnp.concatenate([hi, hi, lo], axis=1),
            jnp.concatenate([t, tlo[f, :, piece].reshape(128, 256), t], axis=0),
            1,
            0,
        )
        hi, lo = halves(c)
        turned = dot(jnp.concatenate([hi, lo, hi], axis=1), uturn[...], 1, 0)
        turned = turned * tab[1 - f, :, piece].reshape(128, 256)
        if f == 0:
            turned = -turned
        for d in range(3):
            n = nb[d, :, piece].reshape(128, 128)
            for side in range(2):
                mine = slice(128 * side, 128 * side + 128)
                cgrad[d, :, mine] += jnp.sum((turned[:, mine] * n).reshape(16, 8, 128), axis=0)

    for off2 in (0,) + rounds:
        for f in range(2):
            for off in rounds:
                waits1[f, off, off2].wait_recv()
            back(f, seconds[f][(4 - off2) % 4])
    xout[0:128, :] = fgrad[:, 128:256]
    for d in range(3):
        xout[128 + 8 * d : 136 + 8 * d, :] = cgrad[d, :, 128:256]
    wait_mate = send(xout, xin, xin, partner)

    def gather(buffer, value, me, to, come, offs):
        buffer[me] = value
        return [
            send(buffer.at[me], buffer.at[me], buffer.at[come(off)], to(off)) for off in offs
        ]

    def add_up(buffer):
        value = buffer[0]
        for i in range(1, 16):
            value = value + buffer[i]
        return value

    fown = fgrad[:, 0:128] + gshort[...]
    wait_uvir.wait_recv()
    for m, (a, b) in enumerate(PAIRS):
        s = jnp.sum(fown * uvir[0, m] + fgrad[:, 128:256] * uvir[1, m], axis=0, keepdims=True)
        s = jnp.sum(s, axis=1, keepdims=True)
        tile = tile + jnp.where((lanes == 3 * a + b) | (lanes == 3 * b + a), s, 0.0)
    waits_v = gather(va, tile, m_zq, among_zq, from_zq, FAR_ZQ)
    wait_mate.wait_recv()

    du = (fown + xin[0:128, :]) * dsilu[...]
    daggregate = dot(wmix[...], du, 1, 0, HIGH)
    basis[...] = dot(w2[...], daggregate, 1, 0, HIGH)

    def radial_back(r, carry):
        rate, grad = carry
        d = basis[pl.ds(pl.multiple_of(r * 8, 8), 8), :] * (-2.0 * rate)
        k = kinds[...]
        chosen = jnp.zeros((SLOTS, 128), F32)
        for s in range(SPECIES):
            chosen = jnp.where(k == s, d[s : s + 1, :], chosen)
        return rate * GROWTH, grad + chosen * expo[r]

    _, slope = lax.fori_loop(
        0, BASIS, radial_back, (jnp.float32(RATE), jnp.zeros((SLOTS, 128), F32)), unroll=4
    )
    spent = []
    for d in range(3):
        g = slope * vec[d]
        vgrad[d] = g
        spent.append(jnp.sum(g, axis=0, keepdims=True))

    rows16 = iota((16, 128), 0)

    def scatter(g, total):
        left = []
        for s in range(4):
            at = pl.ds(g * 4 + s, 1)
            page = lax.shift_right_logical(nbr[0, 0, at, :], 7)
            lines = jnp.concatenate(
                [jnp.where(rows16 == page, vgrad[d, at, :], 0.0) for d in range(3)], axis=0
            )
            left.append(jnp.concatenate(halves(lines), axis=0))
        return total + dot(jnp.concatenate(left, axis=1), marks[g], 1, 1)

    total = lax.fori_loop(0, SLOTS // 4, scatter, jnp.zeros((96, 128), F32), unroll=8)
    tgrad[...] = total[0:48, :] + total[48:96, :]
    for p in range(8):
        for d in range(3):
            gback[p, d : d + 1, :] = tgrad[16 * d + p + 1 : 16 * d + p + 2, :]
    waits_g = [send(gback.at[p], gret.at[7 - p], gret.at[7 - p], ghosts[p]) for p in range(8)]

    for w in waits_v:
        w.wait_recv()
    waits_v = gather(vb, add_up(va), m_xy, among_xy, from_xy, FAR_XY)
    for w in waits_g:
        w.wait_recv()
    left = []
    for d in range(8):
        hi, lo = halves(jnp.concatenate([gret[d], jnp.zeros((8, 128), F32)], axis=0))
        left.append(jnp.concatenate([hi, lo], axis=0))
    back_home = dot(jnp.concatenate(left, axis=1), gmarks[...], 1, 1)
    back_home = back_home[0:16, :] + back_home[16:32, :]
    moved = [
        jnp.sum(
            cgrad[d, :, 0:128] + xin[128 + 8 * d : 136 + 8 * d, :], axis=0, keepdims=True
        )
        for d in range(3)
    ]
    for d in range(3):
        grad = (
            tgrad[16 * d : 16 * d + 1, :]
            - spent[d]
            + moved[d] * (2.0 * math.pi / LENGTHS[d])
            + back_home[d : d + 1, :]
        )
        out[d : d + 1, :] = -grad
    for w in waits_v:
        w.wait_recv()
    out[4:5, :] = add_up(vb) * (1.0 / VOLUME)
    for copy in started:
        copy.wait_send()


def hand_over(result, force, virial):
    for d in range(3):
        force[d, 0] = result[d : d + 1, :]
    for d in range(3):
        virial[d : d + 1, :] = result[4:5, 3 * d : 3 * d + 3]


def per_device(
    positions, species, counts, neighbours, ghost_index, wave_numbers, embedding,
    w_radial, w_mix, w_read, w_out, amplitude, kernel_width, filter_gain,
):
    result = pl.pallas_call(
        kernel,
        out_shape=pltpu.VMEM((8, 128), F32),
        in_specs=[pl.BlockSpec(memory_space=pltpu.HBM)] * 14,
        out_specs=pl.BlockSpec(memory_space=pltpu.VMEM),
        scratch_shapes=[pltpu.VMEM(shape, dtype) for shape, dtype in INPUTS]
        + [pltpu.VMEM(shape, dtype) for _, shape, dtype in SCRATCH]
        + [
            pltpu.SemaphoreType.DMA((N_COPIES,)),
            pltpu.SemaphoreType.DMA((N_COPIES,)),
            pltpu.SemaphoreType.DMA((14,)),
        ],
        compiler_params=pltpu.CompilerParams(collective_id=0, has_side_effects=True),
        name="ewald",
    )(
        positions, species, counts, neighbours, ghost_index, wave_numbers, embedding,
        w_radial, w_mix, w_read, w_out.reshape(1, 128), amplitude.reshape(1, 128),
        kernel_width.reshape(1, 128), filter_gain,
    )
    return pl.pallas_call(
        hand_over,
        out_shape=(
            jax.ShapeDtypeStruct((3, 1, 1, 128), F32),
            jax.ShapeDtypeStruct((3, 3), F32),
        ),
        in_specs=[pl.BlockSpec(memory_space=pltpu.VMEM)],
        out_specs=(
            pl.BlockSpec(memory_space=pltpu.VMEM),
            pl.BlockSpec(memory_space=pltpu.VMEM),
        ),
        name="hand_over",
    )(pltpu.with_memory_space_constraint(result, pltpu.VMEM))


def solution(mesh):
    return jax.shard_map(
        per_device,
        mesh=mesh,
        in_specs=(
            P(None, "row", "col", None),
            P("row", "col", None),
            P("row", "col", None),
            P("row", "col", None, None),
            P("row", "col", None, None),
            P(), P(), P(), P(), P(), P(), P(), P(), P(),
        ),
        out_specs=(P(None, "row", "col", None), P()),
        check_vma=False,
    )
```

```python
import functools
import math

import jax
import jax.numpy as jnp
from jax import lax
from jax.experimental import pallas as pl
from jax.experimental.pallas import tpu as pltpu
from jax.sharding import PartitionSpec as P

CELL_EDGE = 12.0
HEIGHT = 36.0
ROWS = 32
COLS = 8
VOLUME = CELL_EDGE * ROWS * CELL_EDGE * COLS * HEIGHT
LENGTHS = (CELL_EDGE * ROWS, CELL_EDGE * COLS, HEIGHT)
DIRECTIONS = ((-1, -1), (-1, 0), (-1, 1), (0, -1), (0, 1), (1, -1), (1, 0), (1, 1))
RATE = 0.003
GROWTH = 1.6
BASIS = 16
SPECIES = 6
SLOTS = 64
WAVES = 1000
HIGH = lax.Precision.HIGH
HIGHEST = lax.Precision.HIGHEST
MESH = pl.DeviceIdType.MESH
F32 = jnp.float32
BF16 = jnp.bfloat16
SINE = (
    6.2831854820251465,
    -41.34170150756836,
    81.60513305664062,
    -76.70301818847656,
    42.02592849731445,
    -14.899847030639648,
    3.2381374835968018,
)
COSINE = (
    1.0,
    -19.73920440673828,
    64.93911743164062,
    -85.45014190673828,
    60.16762924194336,
    -25.967599868774414,
    6.528658390045166,
)
def dot(a, b, ca, cb, precision=None):
    return lax.dot_general(
        a, b, (((ca,), (cb,)), ((), ())), precision=precision, preferred_element_type=F32
    )


def horner(coefs, w):
    value = jnp.full_like(w, coefs[-1])
    for c in coefs[-2::-1]:
        value = value * w + c
    return value


def halves(x):
    hi = x.astype(BF16)
    lo = (x - hi.astype(F32)).astype(BF16)
    return hi, lo


def iota(shape, dim):
    return lax.broadcasted_iota(jnp.int32, shape, dim)


N_COPIES = 132
FAR_ZQ = (9, 8, 7, 6, 11, 10, 5, 4, 13, 12, 3, 2, 15, 14, 1)
FAR_XY = (10, 9, 11, 6, 14, 5, 7, 13, 15, 8, 2, 4, 12, 1, 3)
PAIRS = ((0, 0), (0, 1), (0, 2), (1, 1), (1, 2), (2, 2))
INPUTS = (
    ((3, 1, 1, 128), F32), ((1, 1, 128), jnp.int32), ((1, 1, 128), jnp.int32),
    ((1, 1, 64, 128), jnp.int32), ((1, 1, 8, 128), jnp.int32), ((3, 1000), jnp.int32),
    ((6, 128), F32), ((16, 128), F32), ((128, 128), F32), ((128, 128), F32), ((1, 128), F32),
    ((1, 128), F32), ((1, 128), F32), ((1000, 128), F32),
)
SCRATCH = (
    ("own", (8, 128), F32), ("mate", (8, 128), F32), ("gsend", (8, 8, 128), F32),
    ("pages", (9, 8, 128), F32), ("gback", (8, 8, 128), F32), ("gret", (8, 8, 128), F32),
    ("nmat", (16, 1024), F32), ("umat", (16, 256), F32), ("tab", (2, 4, 4, 32, 256), F32),
    ("tsplit", (2, 4, 128, 768), BF16), ("thi", (2, 4, 4, 32, 256), BF16),
    ("tlo", (2, 4, 4, 32, 256), BF16), ("nb", (3, 4, 4, 32, 128), F32),
    ("emb8", (8, 128), F32), ("w2", (128, 128), F32),
    ("vec", (3, 64, 128), F32), ("kinds", (64, 128), F32), ("dist", (64, 128), F32),
    ("expo", (16, 64, 128), F32), ("basis", (128, 128), F32), ("upd", (256, 128), F32),
    ("usplit", (768, 128), BF16), ("uturn", (384, 256), BF16),
    ("dsilu", (128, 128), F32), ("gshort", (128, 128), F32),
    ("sums", (2, 4, 4, 32, 128), F32), ("in1", (2, 3, 4, 32, 128), F32),
    ("part", (2, 4, 32, 128), F32), ("in2", (2, 3, 32, 128), F32),
    ("zin", (7, 8, 128), F32), ("zbuf", (64, 128), F32), ("c3", (64, 128), F32),
    ("coef", (2, 4, 4, 32, 128), F32), ("fgrad", (128, 256), F32), ("cgrad", (3, 8, 256), F32),
    ("xout", (152, 128), F32), ("xin", (152, 128), F32),
    ("marks", (16, 128, 512), BF16), ("gmarks", (128, 1024), BF16),
    ("vgrad", (3, 64, 128), F32), ("tgrad", (48, 128), F32),
    ("pair", (6, 64, 128), F32), ("moment", (6, 128, 128), F32),
    ("uvir", (2, 6, 128, 128), F32),
    ("va", (16, 1, 128), F32), ("vb", (16, 1, 128), F32),
)


def kernel(*refs):
    ins, out = refs[:14], refs[14]
    here = refs[15:29]
    named = refs[29 : 29 + len(SCRATCH)]
    ssem, rsem, lsem = refs[29 + len(SCRATCH) :]
    (pos, spec, cnt, nbr, gidx, wn, emb, wrad, wmix, wread, wout, amp, width, gain) = here
    (
        own, mate, gsend, pages, gback, gret, nmat, umat, tab, tsplit, thi, tlo, nb, emb8, w2,
        vec, kinds, dist, expo, basis, upd, usplit, uturn, dsilu, gshort,
        sums, in1, part, in2, zin, zbuf, c3, coef, fgrad, cgrad, xout, xin,
        marks, gmarks, vgrad, tgrad, pair, moment, uvir, va, vb,
    ) = named
    row = lax.axis_index("row")
    col = lax.axis_index("col")
    q = lax.rem(row, 2)
    zl = lax.rem(lax.div(row, 2), 4)
    y = lax.div(row, 8)
    x = lax.rem(col, 4)
    zh = lax.div(col, 4)
    z = zh * 4 + zl

    xs = [x] + [lax.rem(x + off, 4) for off in (1, 2, 3)]
    ys = [y] + [lax.rem(y + off, 4) for off in (1, 2, 3)]
    zs = [z] + [lax.rem(z + off, 8) for off in range(1, 8)]
    z_cols = [lax.div(at, 4) * 4 for at in zs]
    z_rows = [(at - high) * 2 for at, high in zip(zs, z_cols)]
    y_rows = [at * 8 for at in ys]
    cores = [q, 1 - q]
    x_base = z_cols[0]
    y_base = z_rows[0] + q

    up, down = lax.rem(row + 1, ROWS), lax.rem(row + ROWS - 1, ROWS)
    east, west = lax.rem(col + 1, COLS), lax.rem(col + COLS - 1, COLS)
    ghosts = [((down, row, up)[a + 1], (west, col, east)[b + 1]) for a, b in DIRECTIONS]
    partner = (row + 1 - 2 * q, col)

    def along_x(off):
        return (row, x_base + xs[off])

    def along_y(off):
        return (y_rows[off] + y_base, col)

    def along_z(off):
        return (y_rows[0] + z_rows[off] + q, z_cols[off] + x)

    def among_zq(off):
        dz, dq = off // 2, off % 2
        return (y_rows[0] + z_rows[dz] + cores[dq], z_cols[dz] + x)

    def among_xy(off):
        dx, dy = off // 4, off % 4
        return (y_rows[dy] + y_base, x_base + xs[dx])

    m_zq = z * 2 + q
    m_xy = x * 4 + y

    def from_zq(off):
        dz, dq = off // 2, off % 2
        return zs[(8 - dz) % 8] * 2 + cores[dq]

    def from_xy(off):
        dx, dy = off // 4, off % 4
        return xs[(4 - dx) % 4] * 4 + ys[(4 - dy) % 4]

    loads = [pltpu.make_async_copy(ins[i], here[i], lsem.at[i]) for i in range(14)]
    for i in (0, 1, 4, 2, 3, 5, 6, 7, 8, 9, 10, 11, 12, 13):
        loads[i].start()
    barrier = pltpu.get_barrier_semaphore()
    greeted = (
        ghosts + [among_zq(off) for off in FAR_ZQ] + [among_xy(off) for off in FAR_XY]
    )
    for who in greeted:
        pl.semaphore_signal(barrier, inc=1, device_id=who, device_id_type=MESH)

    started = []

    def send(src, dst, landing, who):
        i = len(started)
        copy = pltpu.make_async_remote_copy(
            src_ref=src,
            dst_ref=dst,
            send_sem=ssem.at[i],
            recv_sem=rsem.at[i],
            device_id=who,
            device_id_type=MESH,
        )
        copy.start()
        started.append(copy)
        return pltpu.make_async_remote_copy(
            src_ref=src,
            dst_ref=landing,
            send_sem=ssem.at[i],
            recv_sem=rsem.at[i],
            device_id=who,
            device_id_type=MESH,
        )

    gback[...] = jnp.zeros((8, 8, 128), F32)
    nmat[...] = jnp.zeros((16, 1024), F32)
    umat[...] = jnp.zeros((16, 256), F32)
    emb8[...] = jnp.zeros((8, 128), F32)
    own[...] = jnp.zeros((8, 128), F32)
    for i in (0, 1, 4):
        loads[i].wait()

    for d in range(3):
        own[d : d + 1, :] = pos[d, 0]
    own[3:4, :] = spec[0].astype(F32)
    table = own[...]
    for d in range(8):
        index = jnp.broadcast_to(gidx[0, 0, d : d + 1, :], (8, 128))
        gsend[d] = jnp.take_along_axis(table, index, axis=1, mode="promise_in_bounds")
    pages[0] = table
    pl.semaphore_wait(barrier, len(greeted))
    wait_mate = send(own, mate, mate, partner)
    waits = [
        send(gsend.at[d], pages.at[8 - d], pages.at[8 - d], ghosts[d]) for d in range(8)
    ]

    for i in (2, 3, 5, 6, 7, 8, 9, 10, 11, 12, 13):
        loads[i].wait()
    numbers = wn[...].astype(F32)
    for p in range(3):
        nmat[3 * p : 3 * p + 3, 0:WAVES] = numbers

    emb8[0:SPECIES, :] = emb[...]
    kinds8 = emb8[...]
    for r in range(BASIS):
        w2[8 * r : 8 * r + 8, :] = wrad[r : r + 1, :] * kinds8 * (1.0 / SLOTS)
    onehot = (spec[0] == iota((8, 128), 0)).astype(F32)
    start = dot(onehot, kinds8, 0, 0, HIGHEST)

    wait_mate.wait_recv()
    column = col.astype(F32) * CELL_EDGE
    offsets = (
        (row.astype(F32) * CELL_EDGE, column, 0.0),
        ((row + 1 - 2 * q).astype(F32) * CELL_EDGE, column, 0.0),
    )
    for side, ref in enumerate((own, mate)):
        for d in range(3):
            turn = (ref[d : d + 1, :] + offsets[side][d]) * (1.0 / LENGTHS[d])
            for p in range(3):
                piece = turn.astype(BF16).astype(F32)
                umat[3 * p + d : 3 * p + d + 1, 128 * side : 128 * side + 128] = piece
                turn = turn - piece
    fractions = umat[...].astype(BF16)

    def trig(i, carry):
        block = nmat[:, pl.ds(pl.multiple_of(q * 512 + i * 128, 128), 128)].astype(BF16)
        turns = dot(block, fractions, 0, 0)
        turns = turns - jnp.floor(turns + 0.5)
        w = turns * turns
        for f, value in enumerate((horner(COSINE, w), horner(SINE, w) * turns)):
            tab[f, i] = value.reshape(4, 32, 256)
            hi, lo = halves(value)
            thi[f, i] = hi.reshape(4, 32, 256)
            tlo[f, i] = lo.reshape(4, 32, 256)
            for side in range(2):
                mine = slice(128 * side, 128 * side + 128)
                for p, half in enumerate((hi, lo, hi)):
                    at = 384 * side + 128 * p
                    tsplit[f, i, :, at : at + 128] = half[:, mine]
        for d in range(3):
            nb[d, i] = dot(block, (iota((16, 128), 0) == d).astype(F32).astype(BF16), 0, 0).reshape(
                4, 32, 128
            )
        return carry

    lax.fori_loop(0, 4, trig, 0)

    for w in waits:
        w.wait_recv()
    live = cnt[0]
    rows8 = iota((8, 128), 0)

    def edge(g, carry):
        at = pl.multiple_of(g * 8, 8)
        index = nbr[0, 0, pl.ds(at, 8), :]
        page = lax.shift_right_logical(index, 7)
        lane = lax.bitwise_and(index, 127)
        picked = [jnp.zeros((8, 128), F32)] * 4
        for p in range(9):
            here = page == p
            for d in range(4):
                line = pages[p, d : d + 1, :]
                if p > 0 and d < 2 and DIRECTIONS[p - 1][d]:
                    line = line + CELL_EDGE * DIRECTIONS[p - 1][d]
                found = jnp.take_along_axis(
                    jnp.broadcast_to(line, (8, 128)), lane, axis=1, mode="promise_in_bounds"
                )
                picked[d] = jnp.where(here, found, picked[d])
        square = jnp.zeros((8, 128), F32)
        for d in range(3):
            v = picked[d] - pos[d, 0]
            vec[d, pl.ds(at, 8), :] = v
            square = square + v * v
        dist[pl.ds(at, 8), :] = square
        kinds[pl.ds(at, 8), :] = jnp.where(rows8 + at < live, picked[3], -1.0)
        return carry

    lax.fori_loop(0, 8, edge, 0, unroll=4)

    def radial(r, rate):
        e = jnp.exp(dist[...] * (-rate))
        expo[r] = e
        k = kinds[...]
        tile = jnp.zeros((8, 128), F32)
        for s in range(SPECIES):
            total = jnp.sum(jnp.where(k == s, e, 0.0), axis=0, keepdims=True)
            tile = jnp.where(rows8 == s, total, tile)
        basis[pl.ds(pl.multiple_of(r * 8, 8), 8), :] = tile
        return rate * GROWTH

    lax.fori_loop(0, BASIS, radial, jnp.float32(RATE), unroll=8)

    aggregate = dot(basis[...], w2[...], 0, 0, HIGH)
    u = dot(aggregate, wmix[...], 1, 0, HIGH)
    gate = 1.0 / (1.0 + jnp.exp(-u))
    mine = start + u * gate
    upd[0:128, :] = mine
    wait_mate = send(upd.at[0:128], upd.at[128:256], upd.at[128:256], partner)
    dsilu[...] = (gate * (1.0 + u * (1.0 - gate))).T
    p = dot(mine, wread[...], 1, 0, HIGH)
    gate = 1.0 / (1.0 + jnp.exp(-p))
    gshort[...] = dot(wread[...], wout[...] * (gate * (1.0 + p * (1.0 - gate))), 1, 1, HIGH)

    def split(side):
        value = upd[128 * side : 128 * side + 128, :]
        hi, lo = halves(value)
        for p, half in enumerate((hi, hi, lo)):
            usplit[384 * side + 128 * p : 384 * side + 128 * p + 128, :] = half

    def split_turned(side):
        hi, lo = halves(upd[128 * side : 128 * side + 128, :].T)
        for p, half in enumerate((hi, hi, lo)):
            uturn[128 * p : 128 * p + 128, 128 * side : 128 * side + 128] = half

    split(0)
    for i in range(4):
        lines = jnp.concatenate([tsplit[f, i, :, 0:384] for f in range(2)], axis=0)
        value = dot(lines, usplit[0:384, :], 1, 0).reshape(2, 4, 32, 128)
        for f in range(2):
            sums[f, i] = value[f]
    wait_mate.wait_recv()
    split(1)

    places = (xs, ys)
    seconds = (ys, xs)
    along = (along_x, along_y)
    order = (2, 1, 3, 0)
    waits1 = {}
    for off in order:
        chunks = [places[f][off] for f in range(2)]
        lines = jnp.concatenate([tsplit[f, chunks[f], :, 384:768] for f in range(2)], axis=0)
        value = dot(lines, usplit[384:768, :], 1, 0).reshape(2, 4, 32, 128)
        for f in range(2):
            chunk = chunks[f]
            sums[f, chunk] += value[f]
            if off == 0:
                continue
            for off2 in order:
                waits1[f, off, off2] = send(
                    sums.at[f, chunk, seconds[f][off2]],
                    in1.at[f, off - 1, off2],
                    in1.at[f, off - 1, off2],
                    along[f](off),
                )
    waits2 = {}
    for off2 in order:
        for f in range(2):
            for off in (1, 3, 2):
                waits1[f, off, off2].wait_recv()
            total = (
                sums[f, places[f][0], seconds[f][off2]]
                + in1[f, 0, off2]
                + in1[f, 1, off2]
                + in1[f, 2, off2]
            )
            if off2 == 0:
                zbuf[32 * f : 32 * f + 32, :] = total
                continue
            part[f, off2] = total
            waits2[f, off2] = send(
                part.at[f, off2], in2.at[f, off2 - 1], in2.at[f, off2 - 1], along[1 - f](off2)
            )
    for f in range(2):
        for off2 in (1, 3, 2):
            waits2[f, off2].wait_recv()
        zbuf[32 * f : 32 * f + 32, :] += in2[f, 0] + in2[f, 1] + in2[f, 2]
    waits = []
    for off in (4, 3, 5, 2, 6, 1, 7):
        at = pl.ds(pl.multiple_of(zs[off] * 8, 8), 8)
        waits.append(send(zbuf.at[at], zin.at[off - 1], zin.at[off - 1], along_z(off)))

    first = 512 * q + (1 - zh) * (128 * x + 32 * y) + zh * (128 * y + 32 * x) + 8 * zl
    chosen = (iota((8, 1024), 1) == iota((8, 1024), 0) + first).astype(BF16)
    mine = dot(chosen, nmat[...].astype(BF16), 1, 1)
    k_of = [mine[:, d : d + 1] * (2.0 * math.pi / LENGTHS[d]) for d in range(3)]
    norm = k_of[0] * k_of[0] + k_of[1] * k_of[1] + k_of[2] * k_of[2]
    inside = lax.div(first, WAVES)
    source = pl.multiple_of(first - inside * WAVES, 8)
    weight = amp[...] * gain[pl.ds(source, 8), :] * jnp.exp(-width[...] * norm)
    weight = jnp.where(rows8 + first < WAVES, weight * (1.0 / VOLUME), 0.0)

    rows128 = iota((128, 128), 0)

    def mark(g, carry):
        for s in range(4):
            lane = lax.bitwise_and(nbr[0, 0, pl.ds(g * 4 + s, 1), :], 127)
            marks[g, :, 128 * s : 128 * s + 128] = (rows128 == lane).astype(F32).astype(BF16)
        return carry

    lax.fori_loop(0, 16, mark, 0)
    for d in range(8):
        gmarks[:, 128 * d : 128 * d + 128] = (
            (rows128 == gidx[0, 0, d : d + 1, :]).astype(F32).astype(BF16)
        )

    split_turned(0)
    split_turned(1)
    for m, (a, b) in enumerate(PAIRS):
        pair[m] = vec[a] * vec[b]

    def moments(r, rate):
        e = expo[r] * (2.0 * rate)
        k = kinds[...]
        parts = [jnp.where(k == s, e, 0.0) for s in range(SPECIES)]
        for m in range(6):
            v = pair[m]
            tile = jnp.zeros((8, 128), F32)
            for s in range(SPECIES):
                total = jnp.sum(parts[s] * v, axis=0, keepdims=True)
                tile = jnp.where(rows8 == s, total, tile)
            moment[m, pl.ds(pl.multiple_of(r * 8, 8), 8), :] = tile
        return rate * GROWTH

    lax.fori_loop(0, BASIS, moments, jnp.float32(RATE))

    for w in waits:
        w.wait_recv()
    total = zbuf[pl.ds(pl.multiple_of(z * 8, 8), 8), :]
    for i in range(7):
        total = total + zin[i]
    result = weight * total
    mine_z = pl.ds(pl.multiple_of(z * 8, 8), 8)
    c3[mine_z, :] = result
    waits = []
    for off in (4, 3, 5, 2, 6, 1, 7):
        at = pl.ds(pl.multiple_of(zs[8 - off] * 8, 8), 8)
        waits.append(send(c3.at[mine_z], c3.at[mine_z], c3.at[at], along_z(off)))

    power = result * total
    strain = jnp.sum(width[...] * power, axis=1, keepdims=True)
    energy = 0.5 * jnp.sum(jnp.sum(power, axis=1, keepdims=True), axis=0, keepdims=True)
    lanes = iota((1, 128), 1)
    tile = jnp.where((lanes == 0) | (lanes == 4) | (lanes == 8), energy, 0.0)
    for a, b in PAIRS:
        s = jnp.sum(k_of[a] * k_of[b] * strain, axis=0, keepdims=True)
        tile = tile - jnp.where((lanes == 3 * a + b) | (lanes == 3 * b + a), s, 0.0)

    turned_mix = wmix[...].T
    for m in range(6):
        answer = dot(w2[...], moment[m], 0, 0, HIGH)
        uvir[0, m] = dot(turned_mix, answer, 1, 0, HIGH) * dsilu[...]
    wait_uvir = send(uvir.at[0], uvir.at[1], uvir.at[1], partner)
    fgrad[...] = jnp.zeros((128, 256), F32)
    cgrad[...] = jnp.zeros((3, 8, 256), F32)

    for w in waits:
        w.wait_recv()

    rounds = (1, 3, 2)
    waits2, waits1 = {}, {}

    def spread(f, off2, piece, src):
        for off in (2, 1, 3):
            waits1[f, off, off2] = send(
                src,
                coef.at[f, places[f][0], piece],
                coef.at[f, places[f][4 - off], piece],
                along[f](off),
            )

    for off2 in (2, 1, 3):
        for f in range(2):
            waits2[f, off2] = send(
                c3.at[32 * f : 32 * f + 32],
                coef.at[f, places[f][0], seconds[f][0]],
                coef.at[f, places[f][0], seconds[f][(4 - off2) % 4]],
                along[1 - f](off2),
            )
    for f in range(2):
        spread(f, 0, seconds[f][0], c3.at[32 * f : 32 * f + 32])
        coef[f, places[f][0], seconds[f][0]] = c3[32 * f : 32 * f + 32, :]
    for off2 in rounds:
        for f in range(2):
            waits2[f, off2].wait_recv()
            piece = seconds[f][(4 - off2) % 4]
            spread(f, off2, piece, coef.at[f, places[f][0], piece])

    def back(f, piece):
        c = coef[f, :, piece].reshape(128, 128)
        hi, lo = halves(c.T)
        t = thi[f, :, piece].reshape(128, 256)
        fgrad[...] += dot(
            jnp.concatenate([hi, hi, lo], axis=1),
            jnp.concatenate([t, tlo[f, :, piece].reshape(128, 256), t], axis=0),
            1,
            0,
        )
        hi, lo = halves(c)
        turned = dot(jnp.concatenate([hi, lo, hi], axis=1), uturn[...], 1, 0)
        turned = turned * tab[1 - f, :, piece].reshape(128, 256)
        if f == 0:
            turned = -turned
        for d in range(3):
            n = nb[d, :, piece].reshape(128, 128)
            for side in range(2):
                mine = slice(128 * side, 128 * side + 128)
                cgrad[d, :, mine] += jnp.sum((turned[:, mine] * n).reshape(16, 8, 128), axis=0)

    for off2 in (0,) + rounds:
        for f in range(2):
            for off in rounds:
                waits1[f, off, off2].wait_recv()
            back(f, seconds[f][(4 - off2) % 4])
    xout[0:128, :] = fgrad[:, 128:256]
    for d in range(3):
        xout[128 + 8 * d : 136 + 8 * d, :] = cgrad[d, :, 128:256]
    wait_mate = send(xout, xin, xin, partner)

    def gather(buffer, value, me, to, come, offs):
        buffer[me] = value
        return [
            send(buffer.at[me], buffer.at[me], buffer.at[come(off)], to(off)) for off in offs
        ]

    def add_up(buffer):
        value = buffer[0]
        for i in range(1, 16):
            value = value + buffer[i]
        return value

    fown = fgrad[:, 0:128] + gshort[...]
    wait_uvir.wait_recv()
    for m, (a, b) in enumerate(PAIRS):
        s = jnp.sum(fown * uvir[0, m] + fgrad[:, 128:256] * uvir[1, m], axis=0, keepdims=True)
        s = jnp.sum(s, axis=1, keepdims=True)
        tile = tile + jnp.where((lanes == 3 * a + b) | (lanes == 3 * b + a), s, 0.0)
    waits_v = gather(va, tile, m_zq, among_zq, from_zq, FAR_ZQ)
    wait_mate.wait_recv()

    du = (fown + xin[0:128, :]) * dsilu[...]
    daggregate = dot(wmix[...], du, 1, 0, HIGH)
    basis[...] = dot(w2[...], daggregate, 1, 0, HIGH)

    def radial_back(r, carry):
        rate, grad = carry
        d = basis[pl.ds(pl.multiple_of(r * 8, 8), 8), :] * (-2.0 * rate)
        k = kinds[...]
        chosen = jnp.zeros((SLOTS, 128), F32)
        for s in range(SPECIES):
            chosen = jnp.where(k == s, d[s : s + 1, :], chosen)
        return rate * GROWTH, grad + chosen * expo[r]

    _, slope = lax.fori_loop(
        0, BASIS, radial_back, (jnp.float32(RATE), jnp.zeros((SLOTS, 128), F32)), unroll=8
    )
    spent = []
    for d in range(3):
        g = slope * vec[d]
        vgrad[d] = g
        spent.append(jnp.sum(g, axis=0, keepdims=True))

    rows16 = iota((16, 128), 0)

    def scatter(g, total):
        left = []
        for s in range(4):
            at = pl.ds(g * 4 + s, 1)
            page = lax.shift_right_logical(nbr[0, 0, at, :], 7)
            lines = jnp.concatenate(
                [jnp.where(rows16 == page, vgrad[d, at, :], 0.0) for d in range(3)], axis=0
            )
            left.append(jnp.concatenate(halves(lines), axis=0))
        return total + dot(jnp.concatenate(left, axis=1), marks[g], 1, 1)

    total = lax.fori_loop(0, SLOTS // 4, scatter, jnp.zeros((96, 128), F32), unroll=8)
    tgrad[...] = total[0:48, :] + total[48:96, :]
    for p in range(8):
        for d in range(3):
            gback[p, d : d + 1, :] = tgrad[16 * d + p + 1 : 16 * d + p + 2, :]
    waits_g = [send(gback.at[p], gret.at[7 - p], gret.at[7 - p], ghosts[p]) for p in range(8)]

    for w in waits_v:
        w.wait_recv()
    waits_v = gather(vb, add_up(va), m_xy, among_xy, from_xy, FAR_XY)
    for w in waits_g:
        w.wait_recv()
    left = []
    for d in range(8):
        hi, lo = halves(jnp.concatenate([gret[d], jnp.zeros((8, 128), F32)], axis=0))
        left.append(jnp.concatenate([hi, lo], axis=0))
    back_home = dot(jnp.concatenate(left, axis=1), gmarks[...], 1, 1)
    back_home = back_home[0:16, :] + back_home[16:32, :]
    moved = [
        jnp.sum(
            cgrad[d, :, 0:128] + xin[128 + 8 * d : 136 + 8 * d, :], axis=0, keepdims=True
        )
        for d in range(3)
    ]
    for d in range(3):
        grad = (
            tgrad[16 * d : 16 * d + 1, :]
            - spent[d]
            + moved[d] * (2.0 * math.pi / LENGTHS[d])
            + back_home[d : d + 1, :]
        )
        out[d : d + 1, :] = -grad
    for w in waits_v:
        w.wait_recv()
    out[4:5, :] = add_up(vb) * (1.0 / VOLUME)
    for copy in started:
        copy.wait_send()


def hand_over(result, force, virial):
    for d in range(3):
        force[d, 0] = result[d : d + 1, :]
    for d in range(3):
        virial[d : d + 1, :] = result[4:5, 3 * d : 3 * d + 3]


def per_device(
    positions, species, counts, neighbours, ghost_index, wave_numbers, embedding,
    w_radial, w_mix, w_read, w_out, amplitude, kernel_width, filter_gain,
):
    result = pl.pallas_call(
        kernel,
        out_shape=pltpu.VMEM((8, 128), F32),
        in_specs=[pl.BlockSpec(memory_space=pltpu.HBM)] * 14,
        out_specs=pl.BlockSpec(memory_space=pltpu.VMEM),
        scratch_shapes=[pltpu.VMEM(shape, dtype) for shape, dtype in INPUTS]
        + [pltpu.VMEM(shape, dtype) for _, shape, dtype in SCRATCH]
        + [
            pltpu.SemaphoreType.DMA((N_COPIES,)),
            pltpu.SemaphoreType.DMA((N_COPIES,)),
            pltpu.SemaphoreType.DMA((14,)),
        ],
        compiler_params=pltpu.CompilerParams(collective_id=0, has_side_effects=True),
        name="ewald",
    )(
        positions, species, counts, neighbours, ghost_index, wave_numbers, embedding,
        w_radial, w_mix, w_read, w_out.reshape(1, 128), amplitude.reshape(1, 128),
        kernel_width.reshape(1, 128), filter_gain,
    )
    return pl.pallas_call(
        hand_over,
        out_shape=(
            jax.ShapeDtypeStruct((3, 1, 1, 128), F32),
            jax.ShapeDtypeStruct((3, 3), F32),
        ),
        in_specs=[pl.BlockSpec(memory_space=pltpu.VMEM)],
        out_specs=(
            pl.BlockSpec(memory_space=pltpu.VMEM),
            pl.BlockSpec(memory_space=pltpu.VMEM),
        ),
        name="hand_over",
    )(pltpu.with_memory_space_constraint(result, pltpu.VMEM))


def solution(mesh):
    return jax.shard_map(
        per_device,
        mesh=mesh,
        in_specs=(
            P(None, "row", "col", None),
            P("row", "col", None),
            P("row", "col", None),
            P("row", "col", None, None),
            P("row", "col", None, None),
            P(), P(), P(), P(), P(), P(), P(), P(), P(),
        ),
        out_specs=(P(None, "row", "col", None), P()),
        check_vma=False,
    )
```
